128 devices in a mesh: gy: 16 (over y_hi, z, core), gz: 8 (over x, y_lo).
Axes of the slice: x: 4, y: 4 (y_hi: 2, y_lo: 2; y = y_hi * 2 + y_lo), z: 4, core: 2. Of those that a mesh axis runs over, the one named last changes fastest.
Arguments:
- field_in: bfloat16 [64, 256, 128, 256], P(None, 'gy', 'gz'), may hold values from -42 to 42
- spectral_weight: bfloat16 [32, 32, 32, 64, 128], P('gz', 'gy'), may hold values from -1.5258789e-05 to 1.5258789e-05
- point_weight: bfloat16 [64, 64], replicated, may hold values from -0.75 to 0.75
- point_bias: float32 [64], replicated, may hold values from -3 to 3
- out_weight: bfloat16 [64, 3], replicated, may hold values from -0.75 to 0.75
- out_bias: float32 [3], replicated, may hold values from -4 to 4
Outputs:
- loss_value: float32 [], replicated
- grad_spectral: float32 [32, 32, 32, 64, 128], P('gz', 'gy')
- grad_point: float32 [64, 64], replicated
- grad_point_bias: float32 [64], replicated
- grad_out: float32 [64, 3], replicated
- grad_out_bias: float32 [3], replicated
The draws below stay inside these ranges and needn't reach their ends.
All inputs are finite; a program needn't handle non-finite values.
Results may differ from the reference program's by a relative error of at most 0.01.
Values may be sent and summed in bfloat16 or wider, within the bound.
A program may use at most 192 MiB of HBM per device.

```python
import math
import jax
import jax.numpy as jnp
from jax import lax

C = 64
NX = 256
NY = 256
NZ = 128
MX = 32
MY = 32
MZ = 32
CY = 16
N_GY = 16


def draw_field_in(key, part):
    noise_key, column_key = jax.random.split(key, 2)
    y_pos = jnp.arange(NY, dtype=jnp.float32) / NY
    z_pos = jnp.arange(NZ, dtype=jnp.float32) / NZ
    height_trend = jnp.exp(math.log(6.0) * (y_pos[:, None] - 0.5 + (0.5 - z_pos[None, :])))
    column_scale = jnp.exp(jax.random.uniform(column_key, (NY, NZ), jnp.float32, -0.8, 0.8))
    values = jnp.clip(jax.random.normal(noise_key, (C, NY, NZ, NX), jnp.float32), -2.5, 2.5)
    return (values * (height_trend * column_scale)[None, :, :, None]).astype(jnp.bfloat16)


def shard_levels(rng, shape, shards, low, high):
    def one(dim, parts):
        draws = jax.random.uniform(jax.random.fold_in(jax.random.fold_in(rng, 6), dim), (parts,), jnp.float32, low / len(shards), high / len(shards))
        return jnp.repeat(jnp.exp(draws), shape[dim] // parts).reshape((-1,) + (1,) * (len(shape) - dim - 1))

    factor_of = one(*shards[0])
    for cut in shards[1:]:
        factor_of = factor_of * one(*cut)
    return factor_of


def centred(own_key, dims, scale, limit, pieces=(), kind=jnp.bfloat16):
    gain = shard_levels(own_key, dims, pieces, -0.22, 0.18) if pieces else 1.0
    entries = jax.random.normal(own_key, dims, jnp.float32) * scale * gain
    return jnp.minimum(jnp.maximum(entries, -limit), limit).astype(kind)


def setup_inputs(seed: int = 0) -> dict:
    splits = jax.random.split(jax.random.key(seed), 7)
    return {
        "field_in": draw_field_in(jax.random.fold_in(splits[6], 71), 0),
        "spectral_weight": centred(splits[1], (MZ, MY, MX, C, 2 * C), (2 * C * (MX * MY * MZ) ** 2) ** -0.5, 1.52587890625e-05, ((0, 8), (1, 16))),
        "point_weight": centred(splits[2], (C, C), C ** -0.5, 0.75),
        "point_bias": centred(splits[3], (C,), 0.5, 3.0, (), jnp.float32),
        "out_weight": centred(splits[4], (C, 3), C ** -0.5, 0.75),
        "out_bias": centred(splits[5], (3,), 1.0, 4.0, (), jnp.float32),
    }


def frequencies(first_mode, mode_count, mode_total):
    mode_index = first_mode + jnp.arange(mode_count, dtype=jnp.int32)
    return jnp.where(mode_index < mode_total // 2, mode_index, mode_index - mode_total)

def twiddle(positions, wave_numbers, length):
    product = positions[:, None] * wave_numbers[None, :] % length
    phases = product.astype(jnp.float32) * (2.0 * math.pi / length)
    return (jnp.cos(phases).astype(jnp.bfloat16), jnp.sin(phases).astype(jnp.bfloat16))

def rotate(with_cos, with_sin, forward):
    half_width = with_cos.shape[-1] // 2
    cos_real, cos_imag = (with_cos[..., :half_width], with_cos[..., half_width:])
    sin_real, sin_imag = (with_sin[..., :half_width], with_sin[..., half_width:])
    if forward:
        return jnp.concatenate([cos_real + sin_imag, cos_imag - sin_real], axis=-1)
    return jnp.concatenate([cos_real - sin_imag, cos_imag + sin_real], axis=-1)

def x_tables(length, mode_total):
    cos_part, sin_part = twiddle(jnp.arange(length, dtype=jnp.int32), frequencies(0, mode_total, mode_total), length)
    forward_table = jnp.stack([cos_part, -sin_part], axis=1)
    inverse_table = jnp.stack([cos_part.T, -sin_part.T], axis=0)
    return (forward_table, inverse_table)

def to_modes(x_modes, factor):
    y_cos, y_sin = twiddle(jnp.arange(NY, dtype=jnp.int32), frequencies(0, MY, MY), NY)
    operand = x_modes.astype(jnp.float32)
    with_cos = jnp.einsum('yzkc,yj->jzkc', operand, y_cos.astype(jnp.float32))
    with_sin = jnp.einsum('yzkc,yj->jzkc', operand, y_sin.astype(jnp.float32))
    y_modes = rotate(with_cos, with_sin, True).astype(jnp.bfloat16)
    z_cos, z_sin = twiddle(jnp.arange(NZ, dtype=jnp.int32), frequencies(0, MZ, MZ), NZ)
    operand = y_modes.astype(jnp.float32)
    with_cos = jnp.einsum('bzkc,zj->jbkc', operand, z_cos.astype(jnp.float32))
    with_sin = jnp.einsum('bzkc,zj->jbkc', operand, z_sin.astype(jnp.float32))
    return (rotate(with_cos, with_sin, True) * factor).astype(jnp.bfloat16)

def from_modes(modes_out):
    z_cos, z_sin = twiddle(jnp.arange(NZ, dtype=jnp.int32), frequencies(0, MZ, MZ), NZ)
    operand = modes_out.astype(jnp.float32)
    with_cos = jnp.einsum('jbkc,zj->bzkc', operand, z_cos.astype(jnp.float32))
    with_sin = jnp.einsum('jbkc,zj->bzkc', operand, z_sin.astype(jnp.float32))
    z_back = rotate(with_cos, with_sin, False).astype(jnp.bfloat16)
    y_cos, y_sin = twiddle(jnp.arange(NY, dtype=jnp.int32), frequencies(0, MY, MY), NY)
    operand = z_back.astype(jnp.float32)
    with_cos = jnp.einsum('jzkc,yj->yzkc', operand, y_cos.astype(jnp.float32))
    with_sin = jnp.einsum('jzkc,yj->yzkc', operand, y_sin.astype(jnp.float32))
    return rotate(with_cos, with_sin, False).astype(jnp.bfloat16)

def mix_modes(modes_in, spectral_weight):

    def one_plane(plane_pair):
        plane_in, plane_weight = plane_pair
        channels = plane_weight.shape[-2]
        operand = plane_in.astype(jnp.float32)
        weights_f = plane_weight.astype(jnp.float32)
        with_real = jnp.einsum('bki,bkio->bko', operand[..., :channels], weights_f)
        with_imag = jnp.einsum('bki,bkio->bko', operand[..., channels:], weights_f)
        return jnp.concatenate([with_real[..., :channels] - with_imag[..., channels:], with_real[..., channels:] + with_imag[..., :channels]], axis=-1).astype(jnp.bfloat16)
    return lax.map(one_plane, (modes_in, spectral_weight))

def weight_grad(modes_in, grad_modes):

    def one_plane(plane_pair):
        plane_in, plane_grad = plane_pair
        channels = plane_in.shape[-1] // 2
        operand = plane_in.astype(jnp.float32)
        grads_f = plane_grad.astype(jnp.float32)
        with_real = jnp.einsum('bki,bko->bkio', operand[..., :channels], grads_f)
        with_imag = jnp.einsum('bki,bko->bkio', operand[..., channels:], grads_f)
        return jnp.concatenate([with_real[..., :channels] + with_imag[..., channels:], with_real[..., channels:] - with_imag[..., :channels]], axis=-1)
    return lax.map(one_plane, (modes_in, grad_modes))

def cell_loss(field_b, slope_x, slope_y, slope_z):
    current_x = slope_y[2] - slope_z[1]
    current_y = slope_z[0] - slope_x[2]
    current_z = slope_x[1] - slope_y[0]
    force_x = current_y * field_b[2] - current_z * field_b[1]
    force_y = current_z * field_b[0] - current_x * field_b[2]
    force_z = current_x * field_b[1] - current_y * field_b[0]
    spread = slope_x[0] + slope_y[1] + slope_z[2]
    strength = field_b[0] * field_b[0] + field_b[1] * field_b[1] + field_b[2] * field_b[2] + 1.0
    return (force_x * force_x + force_y * force_y + force_z * force_z) / strength + spread * spread

def loss_total(b_field):
    padded = jnp.pad(b_field, ((0, 0), (1, 1), (1, 1), (1, 1)))
    center = padded[:, 1:-1, 1:-1, 1:-1]
    slope_x = (padded[:, 1:-1, 1:-1, 2:] - padded[:, 1:-1, 1:-1, :-2]) * 0.5
    slope_y = (padded[:, 2:, 1:-1, 1:-1] - padded[:, :-2, 1:-1, 1:-1]) * 0.5
    slope_z = (padded[:, 1:-1, 2:, 1:-1] - padded[:, 1:-1, :-2, 1:-1]) * 0.5
    return jnp.sum(cell_loss(center, slope_x, slope_y, slope_z)) / (NX * NY * NZ)

def gelu_slope(pre_act):
    normal_cdf = 0.5 * (1.0 + lax.erf(pre_act * (1.0 / math.sqrt(2.0))))
    density = jnp.exp(-0.5 * pre_act * pre_act) * (1.0 / math.sqrt(2.0 * math.pi))
    return normal_cdf + pre_act * density

def reference(field_in, spectral_weight, point_weight, point_bias, out_weight, out_bias):
    forward_table, inverse_table = x_tables(NX, MX)
    channels = field_in.shape[0]
    block_ids = jnp.arange(N_GY, dtype=jnp.int32)

    def x_block(block_id):
        part_in = lax.dynamic_slice_in_dim(field_in, block_id * CY, CY, 1).astype(jnp.float32)
        products = jnp.einsum('cyzx,xpk->yzkpc', part_in, forward_table.astype(jnp.float32))
        return products.reshape(CY, NZ, MX, 2 * channels).astype(jnp.bfloat16)
    x_modes = lax.map(x_block, block_ids).reshape(NY, NZ, MX, 2 * channels)
    modes_in = to_modes(x_modes, math.sqrt(MX * MY * MZ / (NX * NY * NZ)))
    modes_out = mix_modes(modes_in, spectral_weight)
    y_back = from_modes(modes_out)

    def dense_block(block_id):
        part_in = lax.dynamic_slice_in_dim(field_in, block_id * CY, CY, 1).astype(jnp.float32)
        part_modes = lax.dynamic_slice_in_dim(y_back, block_id * CY, CY, 0).astype(jnp.float32)
        spectral = jnp.einsum('yzkpc,pkx->cyzx', part_modes.reshape(CY, NZ, MX, 2, channels), inverse_table.astype(jnp.float32))
        pointwise = jnp.einsum('cyzx,co->oyzx', part_in, point_weight.astype(jnp.float32))
        pre_act = spectral + pointwise + point_bias[:, None, None, None]
        hidden = jax.nn.gelu(pre_act, approximate=False).astype(jnp.bfloat16)
        return (part_in, pre_act, hidden)

    def field_block(block_id):
        part_in, pre_act, hidden = dense_block(block_id)
        return jnp.einsum('cyzx,cb->byzx', hidden.astype(jnp.float32), out_weight.astype(jnp.float32)) + out_bias[:, None, None, None]
    b_field = jnp.transpose(lax.map(field_block, block_ids), (1, 0, 2, 3, 4)).reshape(3, NY, NZ, NX)
    loss_value, pullback = jax.vjp(loss_total, b_field)
    grad_b = pullback(jnp.ones_like(loss_value))[0]

    def grad_block(block_id):
        part_in, pre_act, hidden = dense_block(block_id)
        grad_part = lax.dynamic_slice_in_dim(grad_b, block_id * CY, CY, 1)
        weights_f = out_weight.astype(jnp.float32)
        grad_hidden = jnp.zeros_like(pre_act)
        for component in range(3):
            grad_hidden = grad_hidden + weights_f[:, component][:, None, None, None] * grad_part[component][None]
        grad_pre = (grad_hidden * gelu_slope(pre_act)).astype(jnp.bfloat16)
        grad_pre_f = grad_pre.astype(jnp.float32)
        out_part = jnp.einsum('cyzx,byzx->cb', hidden.astype(jnp.float32), grad_part, precision=lax.Precision.HIGHEST)
        out_bias_part = lax.optimization_barrier(jnp.sum(grad_part, axis=(1, 2, 3)))
        point_part = jnp.einsum('iyzx,oyzx->io', part_in, grad_pre_f)
        point_bias_part = lax.optimization_barrier(jnp.sum(grad_pre_f, axis=(1, 2, 3)))
        products = jnp.einsum('cyzx,xpk->yzkpc', grad_pre_f, forward_table.astype(jnp.float32))
        x_part = products.reshape(CY, NZ, MX, 2 * channels).astype(jnp.bfloat16)
        return (point_part, point_bias_part, out_part, out_bias_part, x_part)
    point_parts, point_bias_parts, out_parts, out_bias_parts, x_parts = lax.map(grad_block, block_ids)
    grad_modes = to_modes(x_parts.reshape(NY, NZ, MX, 2 * channels), 1.0)
    grad_spectral = weight_grad(modes_in, grad_modes)
    return (loss_value, grad_spectral, lax.optimization_barrier(jnp.sum(point_parts, axis=0)), lax.optimization_barrier(jnp.sum(point_bias_parts, axis=0)), lax.optimization_barrier(jnp.sum(out_parts, axis=0)), lax.optimization_barrier(jnp.sum(out_bias_parts, axis=0)))
```

```python
import functools
import math

import jax
import jax.numpy as jnp
import numpy as np
from jax import lax
from jax.experimental import pallas as pl
from jax.experimental.pallas import tpu as pltpu
from jax.sharding import PartitionSpec as P

NX, NY, NZ = 256, 256, 128
M = 32
C = 64
GY, GZ = 16, 8
LY, LZ = 16, 16
QZ = 4
F32, BF16 = jnp.float32, jnp.bfloat16
SCALE = math.sqrt(M * M * M / (NX * NY * NZ))
CELLS = NX * NY * NZ
TAIL_SCALE = 0.24
TAIL = (0.08952144314768905, 0.15555677138787463, -0.15417797314110948, 0.6257953656595543, -0.6462531425989838, 0.5546601809863483, -0.12510264575439553)
MESH = pl.DeviceIdType.MESH
ANY = pl.BlockSpec(memory_space=pl.ANY)


def np_table(length):
    mode = np.arange(M)
    wave = np.where(mode < M // 2, mode, mode - M)
    product = (np.arange(length)[:, None] * wave[None, :]) % length
    phases = product.astype(np.float64) * (2.0 * math.pi / length)
    return np.cos(phases), np.sin(phases)


@functools.lru_cache(None)
def tables():
    cos_x, sin_x = np_table(NX)
    forward = np.zeros((40, NX))
    forward[:16] = cos_x[:, :16].T
    forward[16] = cos_x[:, 16]
    forward[17:32] = sin_x[:, 1:16].T
    forward[32] = sin_x[:, 16]
    inverse = np.zeros((40, NX))
    inverse[0:32:2] = forward[:16]
    inverse[1:32:2] = forward[16:32]
    inverse[32] = forward[32]
    cos_y, sin_y = np_table(NY)
    y_rows = np.kron(np.concatenate([cos_y, sin_y], axis=1).T, np.eye(QZ))
    cos_z, sin_z = np_table(NZ)
    z_rows = []
    for table in (cos_z, sin_z):
        cells = table.reshape(GZ, QZ, 4, M)
        for inner in range(4):
            part = cells[:, :, inner, :].reshape(GZ, QZ, GZ, 4)
            full = np.zeros((GZ, 2, 4, 2, GZ, 4, QZ))
            for gs in range(2):
                for ky2 in range(2):
                    full[:, gs, :, ky2, :, gs * 2 + ky2, :] = part.transpose(2, 3, 0, 1)
            z_rows.append(full.reshape(128, 128))
    z_rows = np.stack(z_rows).reshape(2, 4, 128, 128)
    return forward, inverse, y_rows, z_rows


def const(value):
    return jnp.asarray(value, BF16)


NT = (((1,), (1,)), ((), ()))
TN = (((0,), (0,)), ((), ()))


def dot(left, right, dims=(((1,), (0,)), ((), ()))):
    return lax.dot_general(left, right, dims, preferred_element_type=F32)


def whole(shape):
    return pl.BlockSpec(shape, lambda *_: (0,) * len(shape))


def params(limit=56 << 20):
    return pltpu.CompilerParams(vmem_limit_bytes=limit)


def swap_kernel(axis, count, modes, *refs):
    size = len(modes)
    srcs, dsts, sends, recvs = [refs[i * size : i * size + size] for i in range(4)]
    local = refs[4 * size]
    me = lax.axis_index(axis)
    barrier = pltpu.get_barrier_semaphore()
    for step in range(1, count):
        pl.semaphore_signal(
            barrier, inc=1, device_id={axis: (me + step) % count}, device_id_type=MESH
        )
    pl.semaphore_wait(barrier, count - 1)

    def remote(src, dst, send, recv, peer):
        return pltpu.make_async_remote_copy(
            src_ref=src, dst_ref=dst, send_sem=send, recv_sem=recv,
            device_id={axis: peer}, device_id_type=MESH,
        )

    copies, late = [], []
    for index, mode in enumerate(modes):
        src, dst, send, recv = srcs[index], dsts[index], sends[index], recvs[index]
        if mode == "to0":

            @pl.when(me != 0)
            def _(src=src, dst=dst, send=send, recv=recv):
                remote(src, dst.at[me], send.at[0], recv.at[me], 0).start()

            @pl.when(me == 0)
            def _(src=src, dst=dst, index=index):
                pltpu.make_async_copy(src, dst.at[0], local.at[index]).start()

            def finish(src=src, dst=dst, send=send, recv=recv, index=index):
                @pl.when(me != 0)
                def _():
                    remote(src, dst.at[me], send.at[0], recv.at[me], 0).wait_send()

                @pl.when(me == 0)
                def _():
                    pltpu.make_async_copy(src, dst.at[0], local.at[index]).wait()
                    for k in range(1, count):
                        remote(src, dst.at[k], send.at[0], recv.at[k], k).wait_recv()

            late.append(finish)
        elif mode == "from0":

            @pl.when(me == 0)
            def _(src=src, dst=dst, send=send, recv=recv, index=index):
                pltpu.make_async_copy(src.at[0], dst, local.at[index]).start()
                for k in range(1, count):
                    remote(src.at[k], dst, send.at[k], recv.at[0], k).start()

            def finish(src=src, dst=dst, send=send, recv=recv, index=index):
                @pl.when(me == 0)
                def _():
                    pltpu.make_async_copy(src.at[0], dst, local.at[index]).wait()
                    for k in range(1, count):
                        remote(src.at[k], dst, send.at[k], recv.at[0], k).wait_send()

                @pl.when(me != 0)
                def _():
                    remote(src.at[0], dst, send.at[0], recv.at[0], 0).wait_recv()

            late.append(finish)
        else:
            piece = (lambda p, src=src: src.at[p]) if mode == "swap" else (lambda p, src=src: src)
            copies.append(pltpu.make_async_copy(piece(me), dst.at[me], local.at[index]))
            for step in range(1, count):
                peer = (me + step) % count
                copies.append(
                    remote(piece(peer), dst.at[me], send.at[step], recv.at[step], peer)
                )
    for copy in copies:
        copy.start()
    for copy in copies:
        copy.wait()
    for finish in late:
        finish()


def swap(axis, count, collective_id, *operands):
    modes = tuple(mode for mode, _ in operands)
    args = [value for _, value in operands]
    outs = []
    for mode, value in operands:
        shape = value.shape
        if mode in ("all", "to0"):
            shape = (count,) + shape
        elif mode == "from0":
            shape = shape[1:]
        outs.append(jax.ShapeDtypeStruct(shape, value.dtype))
    size = len(args)
    result = pl.pallas_call(
        functools.partial(swap_kernel, axis, count, modes),
        out_shape=outs,
        in_specs=[ANY] * size,
        out_specs=[ANY] * size,
        scratch_shapes=[pltpu.SemaphoreType.DMA((count,))] * (2 * size)
        + [pltpu.SemaphoreType.DMA((size,))],
        compiler_params=pltpu.CompilerParams(
            collective_id=collective_id, has_side_effects=True
        ),
        name=f"swap_{collective_id}",
    )(*args)
    return result if size > 1 else result[0]


def deal_kernel(inward, src, dst, send, recv, local):
    g, h = lax.axis_index("gy"), lax.axis_index("gz")
    owners = [(2 * h + j % 2, j // 2) for j in range(GY)]
    holders = [(k, g // 2) for k in range(GY)]
    targets, sources = (holders, owners) if inward else (owners, holders)
    slot = h * 2 + g % 2 if inward else g

    def is_me(device):
        return jnp.logical_and(device[0] == g, device[1] == h)

    barrier = pltpu.get_barrier_semaphore()
    for device in sources:

        @pl.when(jnp.logical_not(is_me(device)))
        def _(device=device):
            pl.semaphore_signal(
                barrier, inc=1, device_id={"gy": device[0], "gz": device[1]}, device_id_type=MESH
            )

    diagonal = g // 2 == h
    pl.semaphore_wait(barrier, jnp.where(diagonal, GY - 1, GY))

    def outgoing(j):
        return pltpu.make_async_remote_copy(
            src_ref=src.at[j],
            dst_ref=dst.at[slot],
            send_sem=send.at[j],
            recv_sem=recv.at[slot],
            device_id={"gy": targets[j][0], "gz": targets[j][1]},
            device_id_type=MESH,
        )

    def incoming(j):
        return pltpu.make_async_remote_copy(
            src_ref=src.at[j],
            dst_ref=dst.at[j],
            send_sem=send.at[j],
            recv_sem=recv.at[j],
            device_id={"gy": sources[j][0], "gz": sources[j][1]},
            device_id_type=MESH,
        )

    for j in range(GY):
        mine = is_me(targets[j])

        @pl.when(jnp.logical_not(mine))
        def _(j=j):
            outgoing(j).start()

        @pl.when(mine)
        def _(j=j):
            copy = pltpu.make_async_copy(src.at[j], dst.at[slot], local.at[0])
            copy.start()
            copy.wait()

    for j in range(GY):

        @pl.when(jnp.logical_not(is_me(targets[j])))
        def _(j=j):
            outgoing(j).wait_send()

        @pl.when(jnp.logical_not(is_me(sources[j])))
        def _(j=j):
            incoming(j).wait_recv()


def deal(inward, collective_id, src):
    return pl.pallas_call(
        functools.partial(deal_kernel, inward),
        out_shape=jax.ShapeDtypeStruct(src.shape, src.dtype),
        in_specs=[ANY],
        out_specs=ANY,
        scratch_shapes=[pltpu.SemaphoreType.DMA((GY,))] * 2 + [pltpu.SemaphoreType.DMA((1,))],
        compiler_params=pltpu.CompilerParams(
            collective_id=collective_id, has_side_effects=True
        ),
        name=f"deal_{collective_id}",
    )(src)


def emit_rows(rows_ref, out_ref, extra_ref):
    for half in range(2):
        lanes = slice(half * 128, half * 128 + 128)
        for g in range(GY):
            for part in range(2):
                start = (part * GY + g) * 64
                out_ref[g, part, :, lanes] = rows_ref[half, start : start + 64, :].astype(BF16)
        extra_ref[:, lanes] = rows_ref[half, 2048:2112, :].astype(BF16)


def put_rows(rows_ref, start, value):
    for half in range(2):
        rows_ref[half, pl.ds(start, 40, stride=64), :] = value[:, half * 128 : half * 128 + 128]


def x_kernel(field_ref, table_ref, cells_ref, out_ref, extra_ref, stage, rows):
    y = pl.program_id(0)
    for half in range(2):
        lanes = slice(half * 128, half * 128 + 128)
        stage[half] = field_ref[:, 0, :, lanes].astype(F32).reshape(C * LZ, 128)
        for z in range(LZ):
            cells_ref[0, z, :, lanes] = stage[half, pl.ds(z, C, stride=LZ), :].astype(BF16)
    for q in range(QZ):
        block = cells_ref[0, q * 4 : q * 4 + 4].reshape(4 * C, NX)
        put_rows(rows, y * QZ + q, dot(table_ref[...], block, NT))

    @pl.when(y == LY - 1)
    def _():
        emit_rows(rows, out_ref, extra_ref)


def x_transform(field_in):
    forward = const(tables()[0])
    return pl.pallas_call(
        x_kernel,
        grid=(LY,),
        in_specs=[
            pl.BlockSpec((C, 1, LZ, NX), lambda y: (0, y, 0, 0)),
            whole((40, NX)),
        ],
        out_specs=[
            pl.BlockSpec((1, LZ, C, NX), lambda y: (y, 0, 0, 0)),
            whole((GY, 2, 64, NX)),
            whole((64, NX)),
        ],
        out_shape=[
            jax.ShapeDtypeStruct((LY, LZ, C, NX), BF16),
            jax.ShapeDtypeStruct((GY, 2, 64, NX), BF16),
            jax.ShapeDtypeStruct((64, NX), BF16),
        ],
        scratch_shapes=[pltpu.VMEM((2, C * LZ, 128), F32), pltpu.VMEM((2, 40 * 64, 128), F32)],
        compiler_params=params(),
        name="x_transform",
    )(field_in, forward)


def y_kernel(first_ref, src_ref, extra_ref, table_ref, out_ref):
    first = first_ref[0] == 0
    sums = []
    for part in range(2):
        sums.append(dot(table_ref[...], src_ref[:, part].reshape(GY * 64, NX)))
    sums.append(dot(table_ref[...], extra_ref[...].reshape(GY * 64, NX)))
    zero = jnp.zeros((128, NX), F32)
    cc, cs = sums[0][:128], sums[0][128:]
    sc, ss = sums[1][:128], sums[1][128:]
    ec, es = sums[2][:128], sums[2][128:]
    pc, ps = jnp.where(first, zero, sc), jnp.where(first, zero, ss)
    nc, ns = jnp.where(first, sc, cc), jnp.where(first, ss, cs)
    mc, ms = jnp.where(first, ec, -sc), jnp.where(first, es, -ss)
    parts = (cc - ps, -(cs + pc), nc - ms, -(ns + mc))
    for index, part in enumerate(parts):
        out_ref[:, index] = part.astype(BF16).reshape(GZ, 16, NX)


def y_transform(first, rows, extra):
    return pl.pallas_call(
        y_kernel,
        in_specs=[
            pl.BlockSpec(memory_space=pltpu.SMEM),
            pl.BlockSpec(memory_space=pltpu.VMEM),
            pl.BlockSpec(memory_space=pltpu.VMEM),
            pl.BlockSpec(memory_space=pltpu.VMEM),
        ],
        out_specs=pl.BlockSpec(memory_space=pltpu.VMEM),
        out_shape=jax.ShapeDtypeStruct((GZ, 4, 16, NX), BF16),
        compiler_params=params(),
        name="y_transform",
    )(first, rows, extra, const(tables()[2]))


def y_back_kernel(first_ref, src_ref, table_ref, out_ref, extra_ref):
    first = first_ref[0] == 0
    ar, ai, br, bi = [
        src_ref[:, part].reshape(128, NX).astype(F32) for part in range(4)
    ]
    rows = (
        (jnp.where(first, ar, ar + br), jnp.where(first, -ai, -(ai + bi))),
        (jnp.where(first, br, bi - ai), jnp.where(first, -bi, br - ar)),
        (jnp.where(first, -bi, 0.0), jnp.where(first, -br, 0.0)),
    )
    for part, (upper, lower) in enumerate(rows):
        operand = jnp.concatenate([upper, lower], axis=0).astype(BF16)
        result = dot(table_ref[...], operand).astype(BF16).reshape(GY, 64, NX)
        if part < 2:
            out_ref[:, part] = result
        else:
            extra_ref[...] = result


def y_back(first, modes):
    return pl.pallas_call(
        y_back_kernel,
        in_specs=[
            pl.BlockSpec(memory_space=pltpu.SMEM),
            pl.BlockSpec(memory_space=pltpu.VMEM),
            pl.BlockSpec(memory_space=pltpu.VMEM),
        ],
        out_specs=[pl.BlockSpec(memory_space=pltpu.VMEM)] * 2,
        out_shape=[
            jax.ShapeDtypeStruct((GY, 2, 64, NX), BF16),
            jax.ShapeDtypeStruct((GY, 64, NX), BF16),
        ],
        compiler_params=params(),
        name="y_back",
    )(first, modes, const(tables()[2].T))


def z_kernel(factor, src_ref, table_ref, out_ref):
    for m in range(2):
        sums = []
        for p in range(2):
            block = src_ref[:, m * 2 + p].reshape(128, NX)
            pair = []
            for t in range(2):
                total = None
                for inner in range(4):
                    term = dot(table_ref[t, inner], block[:, inner * C : inner * C + C])
                    total = term if total is None else total + term
                pair.append(total)
            sums.append(pair)
        real = sums[0][0] + sums[1][1]
        imag = sums[1][0] - sums[0][1]
        out_ref[:, :, m * 128 : m * 128 + 128] = (
            jnp.concatenate([real, imag], axis=1) * factor
        ).reshape(GY, 8, 128)


def z_transform(modes, factor):
    return pl.pallas_call(
        functools.partial(z_kernel, factor),
        in_specs=[pl.BlockSpec(memory_space=pltpu.VMEM)] * 2,
        out_specs=pl.BlockSpec(memory_space=pltpu.VMEM),
        out_shape=jax.ShapeDtypeStruct((GY, 8, 256), F32),
        compiler_params=params(),
        name="z_transform",
    )(modes, const(tables()[3]))


def z_back_kernel(src_ref, table_ref, out_ref):
    for m in range(2):
        block = src_ref[:, :, m * 128 : m * 128 + 128].reshape(128, 128).astype(BF16)
        real, imag = [], []
        for inner in range(4):
            cos_part = dot(table_ref[0, inner], block)
            sin_part = dot(table_ref[1, inner], block)
            real.append(cos_part[:, :C] - sin_part[:, C:])
            imag.append(cos_part[:, C:] + sin_part[:, :C])
        for p, pieces in enumerate((real, imag)):
            full = jnp.concatenate(pieces, axis=1).astype(BF16)
            out_ref[:, m * 2 + p] = full.reshape(GZ, 16, NX)


def z_back(modes):
    return pl.pallas_call(
        z_back_kernel,
        in_specs=[pl.BlockSpec(memory_space=pltpu.VMEM)] * 2,
        out_specs=pl.BlockSpec(memory_space=pltpu.VMEM),
        out_shape=jax.ShapeDtypeStruct((GZ, 4, 16, NX), BF16),
        compiler_params=params(),
        name="z_back",
    )(modes, const(tables()[3].transpose(0, 1, 3, 2)))


def to_kx(dealt):
    split = dealt.reshape(GY, 4, 2, 2, 2, C)
    plus, minus = split[:, :, :, 0], split[:, :, :, 1]
    order = jnp.concatenate([plus, minus[:1], minus[1:][::-1]], axis=0)
    return order.transpose(1, 2, 0, 3, 4)


def from_kx(modes):
    order = modes.transpose(2, 0, 1, 3, 4)
    minus = jnp.concatenate([order[16:17], order[17:][::-1]], axis=0)
    return jnp.stack([order[:16], minus], axis=3).reshape(GY, 8, 256)


def weight_grad_kernel(u_ref, g_ref, mask_ref, out_ref):
    for block in range(4):
        right = jnp.concatenate([g_ref[block]] * 8, axis=1) * mask_ref[...]
        result = dot(u_ref[block], right, TN)
        for mode in range(8):
            out_ref[0, block * 8 + mode] = result[:, mode * 128 : mode * 128 + 128]


def weight_grad(modes_in, grad_modes):
    u = modes_in.reshape(M, 16, C)
    real, imag = grad_modes[..., 0, :], grad_modes[..., 1, :]
    g = jnp.stack(
        [jnp.concatenate([real, imag], axis=-1), jnp.concatenate([imag, -real], axis=-1)], axis=3
    ).reshape(M, 16, 128)
    mask = const(np.kron(np.eye(8), np.ones((2, 128))))
    return pl.pallas_call(
        weight_grad_kernel,
        grid=(8,),
        in_specs=[
            pl.BlockSpec((4, 16, C), lambda i: (i, 0, 0)),
            pl.BlockSpec((4, 16, 128), lambda i: (i, 0, 0)),
            whole((16, 1024)),
        ],
        out_specs=pl.BlockSpec((1, M, C, 128), lambda i: (i, 0, 0, 0)),
        out_shape=jax.ShapeDtypeStruct((8, M, C, 128), F32),
        compiler_params=params(),
        name="weight_grad",
    )(u, g, mask)


def normal_parts(value):
    size = jnp.abs(value)
    decay = jnp.exp(-0.5 * value * value)
    t = 1.0 / (1.0 + TAIL_SCALE * size)
    poly = jnp.full_like(value, TAIL[-1])
    for coefficient in TAIL[-2::-1]:
        poly = poly * t + coefficient
    tail = poly * t * decay
    return jnp.where(value < 0.0, tail, 1.0 - tail), decay * (1.0 / math.sqrt(2.0 * math.pi))


def dense_kernel(
    rows_ref, odd_ref, cells_ref, table_ref, point_ref, bias_ref, out_w_ref, out_b_ref,
    hidden_ref, slope_ref, field_ref, low_ref, high_ref, corner_ref, rows,
):
    y = pl.program_id(0)

    @pl.when(y == 0)
    def _():
        corner_ref[...] = jnp.zeros_like(corner_ref)
        for half in range(2):
            lanes = slice(half * 128, half * 128 + 128)
            for g in range(GY * 2):
                rows[half, g * 64 : g * 64 + 64, :] = rows_ref[g, :, lanes].astype(F32)
            rows[half, 2048:2112, :] = odd_ref[:, lanes].astype(F32)
            rows[half, 2112:2560, :] = jnp.zeros((448, 128), F32)

    def quad(q, carry):
        picked = jnp.concatenate(
            [rows[half, pl.ds(y * QZ + q, 40, stride=64), :] for half in range(2)], axis=1
        ).astype(BF16)
        spectral = dot(picked, table_ref[...], TN)
        for inner in range(4):
            z = q * 4 + inner
            pre = (
                spectral[inner * C : inner * C + C]
                + dot(point_ref[...], cells_ref[0, z])
                + bias_ref[...]
            )
            normal_cdf, density = normal_parts(pre)
            hidden = (pre * normal_cdf).astype(BF16)
            hidden_ref[0, z] = hidden
            slope_ref[0, z] = (normal_cdf + pre * density).astype(BF16)
            b_rows = dot(out_w_ref[...], hidden)
            for b in range(3):
                field_ref[b, 0, pl.ds(z, 1), :] = b_rows[b : b + 1] + out_b_ref[b]
        return carry

    lax.fori_loop(0, QZ, quad, 0)
    for b in range(3):
        for i in range(2):
            z = LZ - 2 + i
            low_ref[b, pl.ds(y * 2 + i, 1), :] = field_ref[b, 0, i : i + 1, :]
            high_ref[b, pl.ds(y * 2 + i, 1), :] = field_ref[b, 0, z : z + 1, :]
    for y_edge in range(2):

        @pl.when(y == y_edge * (LY - 1))
        def _(y_edge=y_edge):
            for b in range(3):
                for z_edge in range(2):
                    z = z_edge * (LZ - 1)
                    corner_ref[y_edge * 2 + z_edge, b : b + 1, :] = field_ref[b, 0, z : z + 1, :]


def dense(rows, odd, cells, point_weight, point_bias, out_weight, out_bias):
    out_w = jnp.pad(out_weight.T, ((0, 5), (0, 0)))
    cell_spec = pl.BlockSpec((1, LZ, C, NX), lambda y: (y, 0, 0, 0))
    cell_shape = jax.ShapeDtypeStruct((LY, LZ, C, NX), BF16)
    return pl.pallas_call(
        dense_kernel,
        grid=(LY,),
        in_specs=[
            whole((GY * 2, 64, NX)),
            whole((64, NX)),
            cell_spec,
            whole((40, NX)),
            whole((C, C)),
            whole((C, 1)),
            whole((8, C)),
            pl.BlockSpec(memory_space=pltpu.SMEM),
        ],
        out_specs=[
            cell_spec,
            cell_spec,
            pl.BlockSpec((3, 1, LZ, NX), lambda y: (0, y, 0, 0)),
            whole((3, 32, NX)),
            whole((3, 32, NX)),
            whole((4, 8, NX)),
        ],
        out_shape=[
            cell_shape,
            cell_shape,
            jax.ShapeDtypeStruct((3, LY, LZ, NX), F32),
            jax.ShapeDtypeStruct((3, 32, NX), F32),
            jax.ShapeDtypeStruct((3, 32, NX), F32),
            jax.ShapeDtypeStruct((4, 8, NX), F32),
        ],
        scratch_shapes=[pltpu.VMEM((2, 40 * 64, 128), F32)],
        compiler_params=params(),
        name="dense",
    )(
        rows.reshape(GY * 2, 64, NX),
        odd,
        cells,
        const(tables()[1]),
        point_weight.T,
        point_bias[:, None],
        out_w,
        out_bias,
    )


def grad_kernel(
    hidden_ref, slope_ref, cells_ref, grad_ref, table_ref, out_w_ref,
    rows_ref, odd_ref, point_ref, bias_ref, out_ref,
    stage, rows, point_sum, bias_sum, out_sum,
):
    y = pl.program_id(0)

    @pl.when(y == 0)
    def _():
        point_sum[...] = jnp.zeros_like(point_sum)
        bias_sum[...] = jnp.zeros_like(bias_sum)
        out_sum[...] = jnp.zeros_like(out_sum)

    def quad(q, carry):
        for inner in range(4):
            z = q * 4 + inner
            grad = jnp.concatenate(
                [grad_ref[b, 0, pl.ds(z, 1), :] for b in range(3)] + [jnp.zeros((5, NX), F32)],
                axis=0,
            )
            upper = grad.astype(BF16)
            lower = (grad - upper.astype(F32)).astype(BF16)
            both = jnp.concatenate([upper, lower], axis=0)
            grad_hidden = dot(out_w_ref[...], both)
            stage[inner * C : inner * C + C, :] = (
                grad_hidden * slope_ref[0, z].astype(F32)
            ).astype(BF16)
            out_sum[...] += dot(both, hidden_ref[0, z], NT)
        block = stage[...]
        x_rows = dot(table_ref[...], block, NT)
        put_rows(rows, y * QZ + q, x_rows)
        bias_sum[...] += x_rows[0:8]
        cells = cells_ref[0, pl.ds(q * 4, 4)].reshape(4 * C, NX)
        point_sum[...] += dot(cells, block, NT)
        return carry

    lax.fori_loop(0, QZ, quad, 0)

    @pl.when(y == LY - 1)
    def _():
        emit_rows(rows, rows_ref, odd_ref)
        total = point_sum[0:C, 0:C]
        bias = bias_sum[0:1, 0:C]
        for inner in range(1, 4):
            span = slice(inner * C, inner * C + C)
            total = total + point_sum[span, span]
            bias = bias + bias_sum[0:1, span]
        point_ref[...] = total
        bias_ref[...] = bias
        out_ref[...] = out_sum[0:8] + out_sum[8:16]


def grad_dense(hidden, slope, cells, grad_b, out_weight):
    forward = const(tables()[0])
    out_w = jnp.pad(out_weight, ((0, 0), (0, 5)))
    out_w = jnp.concatenate([out_w, out_w], axis=1)
    cell_spec = pl.BlockSpec((1, LZ, C, NX), lambda y: (y, 0, 0, 0))
    return pl.pallas_call(
        grad_kernel,
        grid=(LY,),
        in_specs=[
            cell_spec,
            cell_spec,
            cell_spec,
            pl.BlockSpec((3, 1, LZ, NX), lambda y: (0, y, 0, 0)),
            whole((40, NX)),
            whole((C, 16)),
        ],
        out_specs=[
            whole((GY, 2, 64, NX)),
            whole((64, NX)),
            whole((C, C)),
            whole((1, C)),
            whole((8, C)),
        ],
        out_shape=[
            jax.ShapeDtypeStruct((GY, 2, 64, NX), BF16),
            jax.ShapeDtypeStruct((64, NX), BF16),
            jax.ShapeDtypeStruct((C, C), F32),
            jax.ShapeDtypeStruct((1, C), F32),
            jax.ShapeDtypeStruct((8, C), F32),
        ],
        scratch_shapes=[
            pltpu.VMEM((4 * C, NX), BF16),
            pltpu.VMEM((2, 40 * 64, 128), F32),
            pltpu.VMEM((4 * C, 4 * C), F32),
            pltpu.VMEM((8, NX), F32),
            pltpu.VMEM((16, C), F32),
        ],
        compiler_params=params(),
        name="grad_dense",
    )(hidden, slope, cells, grad_b, forward, out_w)


DIRECTIONS = [(dy, dz) for dy in (-1, 0, 1) for dz in (-1, 0, 1) if dy or dz]


def halo_kernel(
    field, low, high, corner, y_low, y_high, z_low, z_high, corner_out, send, recv
):
    g, h = lax.axis_index("gy"), lax.axis_index("gz")

    def piece(dy, dz):
        if dz == 0:
            start = LY - 2 if dy > 0 else 0
            return field.at[:, pl.ds(start, 2)], (y_low if dy > 0 else y_high)
        if dy == 0:
            return (high, z_low) if dz > 0 else (low, z_high)
        index = (2 if dy > 0 else 0) + (1 if dz > 0 else 0)
        return corner.at[index], corner_out.at[3 - index]

    def exists(dy, dz):
        y, z = g + dy, h + dz
        return jnp.logical_and(
            jnp.logical_and(y >= 0, y < GY), jnp.logical_and(z >= 0, z < GZ)
        )

    def copy(index):
        dy, dz = DIRECTIONS[index]
        src, dst = piece(dy, dz)
        return pltpu.make_async_remote_copy(
            src_ref=src, dst_ref=dst, send_sem=send.at[index], recv_sem=recv.at[index],
            device_id={"gy": g + dy, "gz": h + dz}, device_id_type=MESH,
        )

    barrier = pltpu.get_barrier_semaphore()
    for dy, dz in DIRECTIONS:

        @pl.when(exists(dy, dz))
        def _(dy=dy, dz=dz):
            pl.semaphore_signal(
                barrier, inc=1, device_id={"gy": g + dy, "gz": h + dz}, device_id_type=MESH
            )

    y_sides = jnp.where(g > 0, 1, 0) + jnp.where(g < GY - 1, 1, 0)
    z_sides = jnp.where(h > 0, 1, 0) + jnp.where(h < GZ - 1, 1, 0)
    pl.semaphore_wait(barrier, (y_sides + 1) * (z_sides + 1) - 1)
    for index in range(8):

        @pl.when(exists(*DIRECTIONS[index]))
        def _(index=index):
            copy(index).start()

    for index in range(8):
        dy, dz = DIRECTIONS[index]

        @pl.when(exists(dy, dz))
        def _(index=index):
            copy(index).wait_send()

        @pl.when(exists(-dy, -dz))
        def _(index=index):
            copy(index).wait_recv()


def halo(collective_id, field, low, high, corner):
    side = jax.ShapeDtypeStruct((3, 2, LZ, NX), F32)
    edge = jax.ShapeDtypeStruct((3, 32, NX), F32)
    return pl.pallas_call(
        halo_kernel,
        out_shape=[side, side, edge, edge, jax.ShapeDtypeStruct((4, 8, NX), F32)],
        in_specs=[ANY] * 4,
        out_specs=[ANY] * 5,
        scratch_shapes=[pltpu.SemaphoreType.DMA((8,))] * 2,
        compiler_params=pltpu.CompilerParams(
            collective_id=collective_id, has_side_effects=True
        ),
        name="halo",
    )(field, low, high, corner)


def cell_loss(field_b, slope_x, slope_y, slope_z):
    current_x = slope_y[2] - slope_z[1]
    current_y = slope_z[0] - slope_x[2]
    current_z = slope_x[1] - slope_y[0]
    force_x = current_y * field_b[2] - current_z * field_b[1]
    force_y = current_z * field_b[0] - current_x * field_b[2]
    force_z = current_x * field_b[1] - current_y * field_b[0]
    spread = slope_x[0] + slope_y[1] + slope_z[2]
    strength = field_b[0] * field_b[0] + field_b[1] * field_b[1] + field_b[2] * field_b[2] + 1.0
    return (force_x * force_x + force_y * force_y + force_z * force_z) / strength + spread * spread


def stencil_kernel(
    place_ref, field_ref, y_low_ref, y_high_ref, z_low_ref, z_high_ref, corner_ref,
    grad_ref, loss_ref, bias_ref, wide, own, slopes,
):
    g, h = place_ref[0], place_ref[1]
    zero_rows = jnp.zeros((8, NX), F32)

    def kept(present, value):
        return jnp.where(present, value, jnp.zeros_like(value))

    for b in range(3):
        wide[b, 2:18, 8:24, :] = field_ref[b]
        wide[b, 0:2, 8:24, :] = kept(g > 0, y_low_ref[b])
        wide[b, 18:20, 8:24, :] = kept(g < GY - 1, y_high_ref[b])
        for plane in (0, 1, 18, 19):
            wide[b, plane, 0:8, :] = zero_rows
            wide[b, plane, 24:32, :] = zero_rows
        for y in range(LY):
            wide[b, y + 2, 0:8, :] = zero_rows
            wide[b, y + 2, 24:32, :] = zero_rows
            wide[b, y + 2, 6:8, :] = kept(h > 0, z_low_ref[b, 2 * y : 2 * y + 2, :])
            wide[b, y + 2, 24:26, :] = kept(h < GZ - 1, z_high_ref[b, 2 * y : 2 * y + 2, :])
        for index in range(4):
            y_side = g < GY - 1 if index // 2 else g > 0
            z_side = h < GZ - 1 if index % 2 else h > 0
            row = 24 if index % 2 else 7
            wide[b, 18 if index // 2 else 1, row : row + 1, :] = kept(
                jnp.logical_and(y_side, z_side), corner_ref[index, b : b + 1, :]
            )
    lane = lax.broadcasted_iota(jnp.int32, (32, NX), 1)
    row = lax.broadcasted_iota(jnp.int32, (32, NX), 0)
    z_cell = h * LZ + row - 8
    weight = jnp.where((z_cell >= 0) & (z_cell < NZ), 1.0 / CELLS, 0.0).astype(F32)
    inner = (row >= 8) & (row < 24)

    def x_diff(value):
        after = jnp.where(lane == NX - 1, 0.0, pltpu.roll(value, NX - 1, 1))
        before = jnp.where(lane == 0, 0.0, pltpu.roll(value, 1, 1))
        return (after - before) * 0.5

    def z_diff(value):
        return (pltpu.roll(value, 31, 0) - pltpu.roll(value, 1, 0)) * 0.5

    def one(plane, loss):
        cells = tuple(wide[b, plane] for b in range(3))
        slope_x = tuple(x_diff(value) for value in cells)
        slope_y = tuple((wide[b, plane + 1] - wide[b, plane - 1]) * 0.5 for b in range(3))
        slope_z = tuple(z_diff(value) for value in cells)
        terms, pullback = jax.vjp(cell_loss, cells, slope_x, slope_y, slope_z)
        y_cell = g * LY + plane - 2
        y_inside = jnp.logical_and(y_cell >= 0, y_cell < NY)
        grad_own, grad_x, grad_y, grad_z = pullback(jnp.where(y_inside, weight, 0.0))
        for b in range(3):
            own[b, plane - 1] = grad_own[b] - x_diff(grad_x[b]) - z_diff(grad_z[b])
            slopes[b, plane - 1] = grad_y[b]
        counted = jnp.logical_and(plane >= 2, plane < 18)
        return loss + jnp.where(jnp.logical_and(inner, counted), terms, 0.0)

    loss = lax.fori_loop(1, 19, one, jnp.zeros((32, NX), F32))
    loss_ref[...] = loss

    def finish(y, sums):
        result = []
        for b in range(3):
            grad = own[b, y + 1, 8:24, :] + (
                slopes[b, y, 8:24, :] - slopes[b, y + 2, 8:24, :]
            ) * 0.5
            grad_ref[b, y] = grad
            result.append(sums[b] + grad)
        return tuple(result)

    sums = lax.fori_loop(0, LY, finish, tuple(jnp.zeros((LZ, NX), F32) for _ in range(3)))
    for b in range(3):
        bias_ref[b] = sums[b]


def stencil(place, field, *halos):
    vmem = pl.BlockSpec(memory_space=pltpu.VMEM)
    return pl.pallas_call(
        stencil_kernel,
        in_specs=[pl.BlockSpec(memory_space=pltpu.SMEM)] + [vmem] * 6,
        out_specs=[vmem] * 3,
        out_shape=[
            jax.ShapeDtypeStruct((3, LY, LZ, NX), F32),
            jax.ShapeDtypeStruct((32, NX), F32),
            jax.ShapeDtypeStruct((3, LZ, NX), F32),
        ],
        scratch_shapes=[
            pltpu.VMEM((3, 20, 32, NX), F32),
            pltpu.VMEM((3, 18, 32, NX), F32),
            pltpu.VMEM((3, 18, 32, NX), F32),
        ],
        compiler_params=params(),
        name="stencil",
    )(place, field, *halos)


def on_device(field_in, spectral_weight, point_weight, point_bias, out_weight, out_bias):
    first = lax.axis_index("gy").astype(jnp.int32).reshape(1)
    place = jnp.stack([lax.axis_index("gy"), lax.axis_index("gz")]).astype(jnp.int32)
    cells, rows, odd = x_transform(field_in)
    rows, odd = swap("gy", GY, 1, ("swap", rows), ("to0", odd))
    modes = swap("gz", GZ, 2, ("swap", y_transform(first, rows, odd)))
    modes_in = to_kx(deal(False, 3, z_transform(modes, SCALE)).astype(BF16))

    mixed = jnp.einsum(
        "abkpi,abkio->abkpo", modes_in, spectral_weight, preferred_element_type=F32
    )
    real = mixed[..., 0, :C] - mixed[..., 1, C:]
    imag = mixed[..., 0, C:] + mixed[..., 1, :C]
    modes_out = jnp.stack([real, imag], axis=3)

    back = z_back(deal(True, 4, from_kx(modes_out)))
    rows, odd = y_back(first, swap("gz", GZ, 5, ("swap", back)))
    rows, odd = swap("gy", GY, 6, ("swap", rows), ("from0", odd))

    hidden, slope, field_b, *edges = dense(
        rows, odd, cells, point_weight, point_bias, out_weight, out_bias
    )
    grad_b, loss_rows, bias_rows = stencil(place, field_b, *halo(10, field_b, *edges))
    rows, odd, point_part, point_bias_part, out_part = grad_dense(
        hidden, slope, cells, grad_b, out_weight
    )
    small = jnp.concatenate(
        [
            jnp.sum(loss_rows).reshape(1),
            jnp.sum(bias_rows, axis=(1, 2)),
            point_bias_part[0],
            out_part[:3].reshape(-1),
        ]
    )
    small = jnp.concatenate(
        [point_part.reshape(32, 128), jnp.pad(small, (0, 1024 - 260)).reshape(8, 128)]
    )
    rows, odd, small = swap("gy", GY, 7, ("swap", rows), ("to0", odd), ("all", small))
    modes, small = swap(
        "gz", GZ, 8, ("swap", y_transform(first, rows, odd)), ("all", jnp.sum(small, axis=0))
    )
    small = jnp.sum(small, axis=0)
    grad_modes = to_kx(deal(False, 9, z_transform(modes, 1.0)).astype(BF16))
    grad_spectral = weight_grad(modes_in, grad_modes).reshape(4, 2, M, C, 2 * C)
    grad_point = small[:32].reshape(C, C)
    rest = small[32:].reshape(-1)
    return (
        rest[0] / CELLS,
        grad_spectral,
        grad_point,
        rest[4:68],
        rest[68:260].reshape(3, C).T,
        rest[1:4],
    )


def solution(mesh):
    return jax.shard_map(
        on_device,
        mesh=mesh,
        in_specs=(P(None, "gy", "gz", None), P("gz", "gy", None, None, None), P(), P(), P(), P()),
        out_specs=(P(), P("gz", "gy", None, None, None), P(), P(), P(), P()),
        check_vma=False,
    )
```

```python
import functools
import math

import jax
import jax.numpy as jnp
import numpy as np
from jax import lax
from jax.experimental import pallas as pl
from jax.experimental.pallas import tpu as pltpu
from jax.sharding import PartitionSpec as P

NX, NY, NZ = 256, 256, 128
M = 32
C = 64
GY, GZ = 16, 8
LY, LZ = 16, 16
YB = 2
QZ = 4
F32, BF16 = jnp.float32, jnp.bfloat16
SCALE = math.sqrt(M * M * M / (NX * NY * NZ))
CELLS = NX * NY * NZ
DENSITY = 1.0 / math.sqrt(math.pi)
MESH = pl.DeviceIdType.MESH
ANY = pl.BlockSpec(memory_space=pl.ANY)


def np_table(length):
    mode = np.arange(M)
    wave = np.where(mode < M // 2, mode, mode - M)
    product = (np.arange(length)[:, None] * wave[None, :]) % length
    phases = product.astype(np.float64) * (2.0 * math.pi / length)
    return np.cos(phases), np.sin(phases)


@functools.lru_cache(None)
def tables():
    cos_x, sin_x = np_table(NX)
    forward = np.zeros((40, NX))
    forward[:16] = cos_x[:, :16].T
    forward[16] = cos_x[:, 16]
    forward[17:32] = sin_x[:, 1:16].T
    forward[32] = sin_x[:, 16]
    inverse = np.zeros((64, NX))
    inverse[33:36] = 1.0
    inverse[0:32:2] = forward[:16]
    inverse[1:32:2] = forward[16:32]
    inverse[32] = forward[32]
    cos_y, sin_y = np_table(NY)
    y_rows = np.kron(np.concatenate([cos_y, sin_y], axis=1).T, np.eye(QZ))
    cos_z, sin_z = np_table(NZ)
    z_rows = []
    for table in (cos_z, sin_z):
        cells = table.reshape(GZ, QZ, 4, M)
        for inner in range(4):
            part = cells[:, :, inner, :].reshape(GZ, QZ, GZ, 4)
            full = np.zeros((GZ, 2, 4, 2, GZ, 4, QZ))
            for gs in range(2):
                for ky2 in range(2):
                    full[:, gs, :, ky2, :, gs * 2 + ky2, :] = part.transpose(2, 3, 0, 1)
            z_rows.append(full.reshape(128, 128))
    z_rows = np.stack(z_rows).reshape(2, 4, 128, 128)
    return forward, inverse, y_rows, z_rows


def const(value):
    return jnp.asarray(value, BF16)


NT = (((1,), (1,)), ((), ()))
TN = (((0,), (0,)), ((), ()))


def dot(left, right, dims=(((1,), (0,)), ((), ()))):
    return lax.dot_general(left, right, dims, preferred_element_type=F32)


def whole(shape):
    return pl.BlockSpec(shape, lambda *_: (0,) * len(shape))


def params(limit=56 << 20):
    return pltpu.CompilerParams(vmem_limit_bytes=limit)


def swap_kernel(axis, count, modes, *refs):
    size = len(modes)
    srcs, dsts, sends, recvs = [refs[i * size : i * size + size] for i in range(4)]
    local = refs[4 * size]
    me = lax.axis_index(axis)
    barrier = pltpu.get_barrier_semaphore()
    for step in range(1, count):
        pl.semaphore_signal(
            barrier, inc=1, device_id={axis: (me + step) % count}, device_id_type=MESH
        )
    pl.semaphore_wait(barrier, count - 1)

    def remote(src, dst, send, recv, peer):
        return pltpu.make_async_remote_copy(
            src_ref=src, dst_ref=dst, send_sem=send, recv_sem=recv,
            device_id={axis: peer}, device_id_type=MESH,
        )

    copies, early, late = [], [], []
    for index, mode in enumerate(modes):
        src, dst, send, recv = srcs[index], dsts[index], sends[index], recvs[index]
        if mode == "to0":

            def begin(step, src=src, dst=dst, send=send, recv=recv):
                @pl.when(jnp.logical_and(me != 0, me == step))
                def _():
                    remote(src, dst.at[me], send.at[0], recv.at[me], 0).start()

            early.append(begin)

            @pl.when(me == 0)
            def _(src=src, dst=dst, index=index):
                pltpu.make_async_copy(src, dst.at[0], local.at[index]).start()

            def finish(src=src, dst=dst, send=send, recv=recv, index=index):
                @pl.when(me != 0)
                def _():
                    remote(src, dst.at[me], send.at[0], recv.at[me], 0).wait_send()

                @pl.when(me == 0)
                def _():
                    pltpu.make_async_copy(src, dst.at[0], local.at[index]).wait()
                    for k in range(1, count):
                        remote(src, dst.at[k], send.at[0], recv.at[k], k).wait_recv()

            late.append(finish)
        elif mode == "from0":

            @pl.when(me == 0)
            def _(src=src, dst=dst, send=send, recv=recv, index=index):
                pltpu.make_async_copy(src.at[0], dst, local.at[index]).start()
                for k in range(1, count):
                    remote(src.at[k], dst, send.at[k], recv.at[0], k).start()

            def finish(src=src, dst=dst, send=send, recv=recv, index=index):
                @pl.when(me == 0)
                def _():
                    pltpu.make_async_copy(src.at[0], dst, local.at[index]).wait()
                    for k in range(1, count):
                        remote(src.at[k], dst, send.at[k], recv.at[0], k).wait_send()

                @pl.when(me != 0)
                def _():
                    remote(src.at[0], dst, send.at[0], recv.at[0], 0).wait_recv()

            late.append(finish)
        else:
            piece = (lambda p, src=src: src.at[p]) if mode == "swap" else (lambda p, src=src: src)
            copies.append((0, pltpu.make_async_copy(piece(me), dst.at[me], local.at[index])))
            for step in range(1, count):
                peer = (me + step) % count
                copies.append(
                    (step, remote(piece(peer), dst.at[me], send.at[step], recv.at[step], peer))
                )
    for step in range(count):
        for at, copy in copies:
            if at == step:
                copy.start()
        for begin in early:
            begin(step)
    copies = [copy for _, copy in copies]
    for copy in copies:
        copy.wait()
    for finish in late:
        finish()


def swap(axis, count, collective_id, *operands):
    modes = tuple(mode for mode, _ in operands)
    args = [value for _, value in operands]
    outs = []
    for mode, value in operands:
        shape = value.shape
        if mode in ("all", "to0"):
            shape = (count,) + shape
        elif mode == "from0":
            shape = shape[1:]
        outs.append(jax.ShapeDtypeStruct(shape, value.dtype))
    size = len(args)
    result = pl.pallas_call(
        functools.partial(swap_kernel, axis, count, modes),
        out_shape=outs,
        in_specs=[ANY] * size,
        out_specs=[ANY] * size,
        scratch_shapes=[pltpu.SemaphoreType.DMA((count,))] * (2 * size)
        + [pltpu.SemaphoreType.DMA((size,))],
        compiler_params=pltpu.CompilerParams(
            collective_id=collective_id, has_side_effects=True
        ),
        name=f"swap_{collective_id}",
    )(*args)
    return result if size > 1 else result[0]


def emit_rows(rows_ref, out_ref, extra_ref):
    for half in range(2):
        lanes = slice(half * 128, half * 128 + 128)
        for g in range(GY):
            for part in range(2):
                start = (part * GY + g) * 64
                out_ref[g, part, :, lanes] = rows_ref[half, start : start + 64, :].astype(BF16)
        extra_ref[:, lanes] = rows_ref[half, 2048:2112, :].astype(BF16)


def put_rows(rows_ref, start, value):
    for half in range(2):
        rows_ref[half, pl.ds(start, 40, stride=64), :] = value[:, half * 128 : half * 128 + 128]


def x_kernel(field_ref, table_ref, cells_ref, out_ref, extra_ref, stage, rows):
    step = pl.program_id(0)

    def plane(k, carry):
        for half in range(2):
            lanes = slice(half * 128, half * 128 + 128)
            stage[half] = field_ref[:, k, :, lanes].astype(F32).reshape(C * LZ, 128)
            for z in range(LZ):
                cells_ref[k, z, :, lanes] = stage[half, pl.ds(z, C, stride=LZ), :].astype(BF16)
        for q in range(QZ):
            block = cells_ref[k, q * 4 : q * 4 + 4].reshape(4 * C, NX)
            put_rows(rows, (step * YB + k) * QZ + q, dot(table_ref[...], block, NT))
        return carry

    lax.fori_loop(0, YB, plane, 0)

    @pl.when(step == LY // YB - 1)
    def _():
        emit_rows(rows, out_ref, extra_ref)


def x_transform(field_in):
    forward = const(tables()[0])
    return pl.pallas_call(
        x_kernel,
        grid=(LY // YB,),
        in_specs=[
            pl.BlockSpec((C, YB, LZ, NX), lambda y: (0, y, 0, 0)),
            whole((40, NX)),
        ],
        out_specs=[
            pl.BlockSpec((YB, LZ, C, NX), lambda y: (y, 0, 0, 0)),
            whole((GY, 2, 64, NX)),
            whole((64, NX)),
        ],
        out_shape=[
            jax.ShapeDtypeStruct((LY, LZ, C, NX), BF16),
            jax.ShapeDtypeStruct((GY, 2, 64, NX), BF16),
            jax.ShapeDtypeStruct((64, NX), BF16),
        ],
        scratch_shapes=[pltpu.VMEM((2, C * LZ, 128), F32), pltpu.VMEM((2, 40 * 64, 128), F32)],
        compiler_params=params(),
        name="x_transform",
    )(field_in, forward)


def y_body(first, src_ref, extra_ref, table_ref, out_ref):
    sums = []
    for part in range(2):
        sums.append(dot(table_ref[...], src_ref[:, part].reshape(GY * 64, NX)))
    sums.append(dot(table_ref[...], extra_ref[...].reshape(GY * 64, NX)))
    zero = jnp.zeros((128, NX), F32)
    cc, cs = sums[0][:128], sums[0][128:]
    sc, ss = sums[1][:128], sums[1][128:]
    ec, es = sums[2][:128], sums[2][128:]
    pc, ps = jnp.where(first, zero, sc), jnp.where(first, zero, ss)
    nc, ns = jnp.where(first, sc, cc), jnp.where(first, ss, cs)
    mc, ms = jnp.where(first, ec, -sc), jnp.where(first, es, -ss)
    parts = (cc - ps, -(cs + pc), nc - ms, -(ns + mc))
    for index, part in enumerate(parts):
        out_ref[:, index] = part.astype(BF16).reshape(GZ, 16, NX)


def y_back_body(first, src_ref, table_ref, out_ref, extra_ref):
    ar, ai, br, bi = [
        src_ref[:, part].reshape(128, NX).astype(F32) for part in range(4)
    ]
    rows = (
        (jnp.where(first, ar, ar + br), jnp.where(first, -ai, -(ai + bi))),
        (jnp.where(first, br, bi - ai), jnp.where(first, -bi, br - ar)),
        (jnp.where(first, -bi, 0.0), jnp.where(first, -br, 0.0)),
    )
    for part, (upper, lower) in enumerate(rows):
        operand = jnp.concatenate([upper, lower], axis=0).astype(BF16)
        result = dot(table_ref[...], operand).astype(BF16).reshape(GY, 64, NX)
        if part < 2:
            out_ref[:, part] = result
        else:
            extra_ref[...] = result


def z_body(factor, src_ref, table_ref, out_ref):
    for m in range(2):
        sums = []
        for p in range(2):
            block = src_ref[:, m * 2 + p].reshape(128, NX)
            pair = []
            for t in range(2):
                total = None
                for inner in range(4):
                    term = dot(table_ref[t, inner], block[:, inner * C : inner * C + C])
                    total = term if total is None else total + term
                pair.append(total)
            sums.append(pair)
        real = sums[0][0] + sums[1][1]
        imag = sums[1][0] - sums[0][1]
        out_ref[:, :, m * 128 : m * 128 + 128] = (
            jnp.concatenate([real, imag], axis=1) * factor
        ).reshape(GY, 8, 128)


def z_back_body(src_ref, table_ref, out_ref):
    for m in range(2):
        block = src_ref[:, :, m * 128 : m * 128 + 128].reshape(128, 128).astype(BF16)
        real, imag = [], []
        for inner in range(4):
            cos_part = dot(table_ref[0, inner], block)
            sin_part = dot(table_ref[1, inner], block)
            real.append(cos_part[:, :C] - sin_part[:, C:])
            imag.append(cos_part[:, C:] + sin_part[:, :C])
        for p, pieces in enumerate((real, imag)):
            full = jnp.concatenate(pieces, axis=1).astype(BF16)
            out_ref[:, m * 2 + p] = full.reshape(GZ, 16, NX)


def mode_places():
    g, h = lax.axis_index("gy"), lax.axis_index("gz")
    owners = [(2 * h + j % 2, j // 2) for j in range(GY)]
    holders = [(k, g // 2) for k in range(GY)]
    return g, h, owners, holders


def greet(g, h, sources, with_gy):
    barrier = pltpu.get_barrier_semaphore()
    for step in range(1, GZ):
        pl.semaphore_signal(
            barrier, inc=1, device_id={"gz": (h + step) % GZ}, device_id_type=MESH
        )
    if with_gy:
        for step in range(1, GY):
            pl.semaphore_signal(
                barrier, inc=1, device_id={"gy": (g + step) % GY}, device_id_type=MESH
            )
    for y, z in sources:

        @pl.when(jnp.logical_not(jnp.logical_and(y == g, z == h)))
        def _(y=y, z=z):
            pl.semaphore_signal(barrier, inc=1, device_id={"gy": y, "gz": z}, device_id_type=MESH)


def await_greetings(g, h, with_gy):
    fixed = GZ - 1 + (GY - 1 if with_gy else 0)
    pl.semaphore_wait(
        pltpu.get_barrier_semaphore(), jnp.where(g // 2 == h, GY - 1, GY) + fixed
    )


def spread(axis, count, me, piece, dst, send, recv, local):
    copies = [pltpu.make_async_copy(piece(me), dst.at[me], local)]
    for step in range(1, count):
        peer = (me + step) % count
        copies.append(
            pltpu.make_async_remote_copy(
                src_ref=piece(peer), dst_ref=dst.at[me],
                send_sem=send.at[step], recv_sem=recv.at[step],
                device_id={axis: peer}, device_id_type=MESH,
            )
        )
    for copy in copies:
        copy.start()
    return copies


def deal(g, h, targets, sources, slot, src, dst, send, recv, local):
    def is_me(device):
        return jnp.logical_and(device[0] == g, device[1] == h)

    def remote(j, device, landing, arrived):
        return pltpu.make_async_remote_copy(
            src_ref=src.at[j], dst_ref=dst.at[landing],
            send_sem=send.at[j], recv_sem=recv.at[arrived],
            device_id={"gy": device[0], "gz": device[1]}, device_id_type=MESH,
        )

    for j in range(GY):
        mine = is_me(targets[j])

        @pl.when(jnp.logical_not(mine))
        def _(j=j):
            remote(j, targets[j], slot, slot).start()

        @pl.when(mine)
        def _(j=j):
            copy = pltpu.make_async_copy(src.at[j], dst.at[slot], local)
            copy.start()
            copy.wait()

    for j in range(GY):

        @pl.when(jnp.logical_not(is_me(targets[j])))
        def _(j=j):
            remote(j, targets[j], slot, slot).wait_send()

        @pl.when(jnp.logical_not(is_me(sources[j])))
        def _(j=j):
            remote(j, sources[j], j, j).wait_recv()


def to_modes_kernel(factor, with_small, *refs):
    if with_small:
        (rows, extra, y_table, z_table, small, dealt, small_out, y_out, z_in, z_out,
         send, recv, send2, recv2, local, small_a, small_b, small_c,
         send3, recv3, send4, recv4) = refs
    else:
        (rows, extra, y_table, z_table, dealt, y_out, z_in, z_out,
         send, recv, send2, recv2, local) = refs
    g, h, owners, holders = mode_places()
    greet(g, h, holders, with_small)
    y_body(g == 0, rows, extra, y_table, y_out)
    if with_small:
        small_a[...] = jnp.sum(small[...], axis=0)
    await_greetings(g, h, with_small)
    copies = spread("gz", GZ, h, lambda p: y_out.at[p], z_in, send, recv, local.at[0])
    if with_small:
        copies += spread("gz", GZ, h, lambda p: small_a, small_b, send3, recv3, local.at[1])
    for copy in copies:
        copy.wait()
    z_body(factor, z_in, z_table, z_out)
    copies = []
    if with_small:
        small_c[...] = jnp.sum(small_b[...], axis=0)
        copies = spread("gy", GY, g, lambda p: small_c, small_out, send4, recv4, local.at[2])
    deal(g, h, owners, holders, g, z_out, dealt, send2, recv2, local.at[3])
    for copy in copies:
        copy.wait()


def to_modes(collective_id, factor, rows, extra, small=None):
    vmem = pl.BlockSpec(memory_space=pltpu.VMEM)
    args = [rows, extra, const(tables()[2]), const(tables()[3])]
    outs = [jax.ShapeDtypeStruct((GY, 8, 256), F32)]
    block = pltpu.VMEM((GZ, 4, 16, NX), BF16)
    gz_sems = [pltpu.SemaphoreType.DMA((GZ,))] * 2
    gy_sems = [pltpu.SemaphoreType.DMA((GY,))] * 2
    scratch = [block, block, pltpu.VMEM((GY, 8, 256), F32)]
    scratch += gz_sems + gy_sems + [pltpu.SemaphoreType.DMA((4,))]
    if small is not None:
        args.append(small)
        outs.append(jax.ShapeDtypeStruct((GY, 8, 128), F32))
        scratch += [
            pltpu.VMEM((8, 128), F32),
            pltpu.VMEM((GZ, 8, 128), F32),
            pltpu.VMEM((8, 128), F32),
        ]
        scratch += gz_sems + gy_sems
    result = pl.pallas_call(
        functools.partial(to_modes_kernel, factor, small is not None),
        out_shape=outs,
        in_specs=[vmem] * len(args),
        out_specs=[ANY] * len(outs),
        scratch_shapes=scratch,
        compiler_params=pltpu.CompilerParams(
            collective_id=collective_id, has_side_effects=True, vmem_limit_bytes=40 << 20
        ),
        name=f"to_modes_{collective_id}",
    )(*args)
    return result if small is not None else result[0]


def from_modes_kernel(
    modes, y_table, z_table, rows, extra, landed, z_out, y_in, send, recv, send2, recv2, local
):
    g, h, owners, holders = mode_places()
    greet(g, h, owners, False)
    await_greetings(g, h, False)
    deal(g, h, holders, owners, h * 2 + g % 2, modes, landed, send2, recv2, local.at[1])
    z_back_body(landed, z_table, z_out)
    copies = spread("gz", GZ, h, lambda p: z_out.at[p], y_in, send, recv, local.at[0])
    for copy in copies:
        copy.wait()
    y_back_body(g == 0, y_in, y_table, rows, extra)


def from_modes(collective_id, modes):
    vmem = pl.BlockSpec(memory_space=pltpu.VMEM)
    block = pltpu.VMEM((GZ, 4, 16, NX), BF16)
    return pl.pallas_call(
        from_modes_kernel,
        out_shape=[
            jax.ShapeDtypeStruct((GY, 2, 64, NX), BF16),
            jax.ShapeDtypeStruct((GY, 64, NX), BF16),
        ],
        in_specs=[vmem] * 3,
        out_specs=[vmem] * 2,
        scratch_shapes=[pltpu.VMEM((GY, 8, 256), F32), block, block]
        + [pltpu.SemaphoreType.DMA((GZ,))] * 2
        + [pltpu.SemaphoreType.DMA((GY,))] * 2
        + [pltpu.SemaphoreType.DMA((2,))],
        compiler_params=pltpu.CompilerParams(
            collective_id=collective_id, has_side_effects=True, vmem_limit_bytes=40 << 20
        ),
        name=f"from_modes_{collective_id}",
    )(modes, const(tables()[2].T), const(tables()[3].transpose(0, 1, 3, 2)))


def to_kx(dealt):
    split = dealt.reshape(GY, 4, 2, 2, 2, C)
    plus, minus = split[:, :, :, 0], split[:, :, :, 1]
    order = jnp.concatenate([plus, minus[:1], minus[1:][::-1]], axis=0)
    return order.transpose(1, 2, 0, 3, 4)


def from_kx(modes):
    order = modes.transpose(2, 0, 1, 3, 4)
    minus = jnp.concatenate([order[16:17], order[17:][::-1]], axis=0)
    return jnp.stack([order[:16], minus], axis=3).reshape(GY, 8, 256)


def weight_grad_kernel(u_ref, g_ref, mask_ref, out_ref):
    for block in range(4):
        right = jnp.concatenate([g_ref[block]] * 8, axis=1) * mask_ref[...]
        result = dot(u_ref[block], right, TN)
        for mode in range(8):
            out_ref[0, block * 8 + mode] = result[:, mode * 128 : mode * 128 + 128]


def weight_grad(modes_in, grad_modes):
    u = modes_in.reshape(M, 16, C)
    real, imag = grad_modes[..., 0, :], grad_modes[..., 1, :]
    g = jnp.stack(
        [jnp.concatenate([real, imag], axis=-1), jnp.concatenate([imag, -real], axis=-1)], axis=3
    ).reshape(M, 16, 128)
    mask = const(np.kron(np.eye(8), np.ones((2, 128))))
    return pl.pallas_call(
        weight_grad_kernel,
        grid=(8,),
        in_specs=[
            pl.BlockSpec((4, 16, C), lambda i: (i, 0, 0)),
            pl.BlockSpec((4, 16, 128), lambda i: (i, 0, 0)),
            whole((16, 1024)),
        ],
        out_specs=pl.BlockSpec((1, M, C, 128), lambda i: (i, 0, 0, 0)),
        out_shape=jax.ShapeDtypeStruct((8, M, C, 128), F32),
        compiler_params=params(),
        name="weight_grad",
    )(u, g, mask)


def dense_kernel(
    rows_ref, odd_ref, cells_ref, table_ref, point_ref, bias_ref, out_w_ref, out_b_ref,
    hidden_ref, slope_ref, field_ref, low_ref, high_ref, corner_ref, rows,
):
    step = pl.program_id(0)

    @pl.when(step == 0)
    def _():
        corner_ref[...] = jnp.zeros_like(corner_ref)
        for half in range(2):
            lanes = slice(half * 128, half * 128 + 128)
            for g in range(GY * 2):
                rows[half, g * 64 : g * 64 + 64, :] = rows_ref[g, :, lanes].astype(F32)
            rows[half, 2048:2112, :] = odd_ref[:, lanes].astype(F32)
            rest = bias_ref[...]
            for part in range(3):
                piece = rest.astype(BF16).astype(F32)
                start = 2112 + part * 64
                rows[half, start : start + 64, :] = jnp.broadcast_to(piece, (64, 128))
                rest = rest - piece
            rows[half, 2304:3072, :] = jnp.zeros((768, 128), F32)

    def plane(k, carry):
        y = step * YB + k
        for q in range(QZ):
            picked = jnp.concatenate(
                [rows[half, pl.ds(y * QZ + q, 48, stride=64), :] for half in range(2)], axis=1
            )
            picked = jnp.concatenate(
                [jnp.zeros((64, NX), F32), picked, jnp.zeros((16, NX), F32)], axis=0
            )
            left = picked.T.astype(BF16)
            for inner in range(4):
                z = q * 4 + inner
                pre = dot(
                    left[inner * C : inner * C + C] + point_ref[...],
                    jnp.concatenate([cells_ref[k, z], table_ref[...]], axis=0),
                )
                scaled = pre * math.sqrt(0.5)
                normal_cdf = 0.5 * lax.erf(scaled) + 0.5
                decay = jnp.exp2(scaled * scaled * -math.log2(math.e))
                hidden = (pre * normal_cdf).astype(BF16)
                hidden_ref[k, z] = hidden
                slope_ref[k, z] = (normal_cdf + scaled * DENSITY * decay).astype(BF16)
                b_rows = dot(out_w_ref[...], hidden)
                for b in range(3):
                    field_ref[b, k, z : z + 1, :] = b_rows[b : b + 1] + out_b_ref[b]
        for b in range(3):
            for i in range(2):
                z = LZ - 2 + i
                low_ref[b, pl.ds(y * 2 + i, 1), :] = field_ref[b, k, i : i + 1, :]
                high_ref[b, pl.ds(y * 2 + i, 1), :] = field_ref[b, k, z : z + 1, :]
        return carry

    lax.fori_loop(0, YB, plane, 0)
    for y_edge in range(2):

        @pl.when(step == y_edge * (LY // YB - 1))
        def _(y_edge=y_edge):
            for b in range(3):
                for z_edge in range(2):
                    z = z_edge * (LZ - 1)
                    corner_ref[y_edge * 2 + z_edge, b : b + 1, :] = field_ref[
                        b, y_edge * (YB - 1), z : z + 1, :
                    ]


def dense(rows, odd, cells, point_weight, point_bias, out_weight, out_bias):
    out_w = jnp.pad(out_weight.T, ((0, 5), (0, 0)))
    cell_spec = pl.BlockSpec((YB, LZ, C, NX), lambda y: (y, 0, 0, 0))
    cell_shape = jax.ShapeDtypeStruct((LY, LZ, C, NX), BF16)
    return pl.pallas_call(
        dense_kernel,
        grid=(LY // YB,),
        in_specs=[
            whole((GY * 2, 64, NX)),
            whole((64, NX)),
            cell_spec,
            whole((64, NX)),
            whole((C, 128)),
            whole((1, 128)),
            whole((8, C)),
            pl.BlockSpec(memory_space=pltpu.SMEM),
        ],
        out_specs=[
            cell_spec,
            cell_spec,
            pl.BlockSpec((3, YB, LZ, NX), lambda y: (0, y, 0, 0)),
            whole((3, 32, NX)),
            whole((3, 32, NX)),
            whole((4, 8, NX)),
        ],
        out_shape=[
            cell_shape,
            cell_shape,
            jax.ShapeDtypeStruct((3, LY, LZ, NX), F32),
            jax.ShapeDtypeStruct((3, 32, NX), F32),
            jax.ShapeDtypeStruct((3, 32, NX), F32),
            jax.ShapeDtypeStruct((4, 8, NX), F32),
        ],
        scratch_shapes=[pltpu.VMEM((2, 48 * 64, 128), F32)],
        compiler_params=params(),
        name="dense",
    )(
        rows.reshape(GY * 2, 64, NX),
        odd,
        cells,
        const(tables()[1]),
        jnp.pad(point_weight.T, ((0, 0), (0, C))),
        jnp.concatenate([point_bias, point_bias])[None],
        out_w,
        out_bias,
    )


def grad_kernel(
    hidden_ref, slope_ref, cells_ref, grad_ref, table_ref, out_w_ref, loss_ref,
    rows_ref, odd_ref, small_ref,
    stage, rows, point_sum, bias_sum, out_sum,
):
    step = pl.program_id(0)

    @pl.when(step == 0)
    def _():
        point_sum[...] = jnp.zeros_like(point_sum)
        bias_sum[...] = jnp.zeros_like(bias_sum)
        out_sum[...] = jnp.zeros_like(out_sum)

    def plane(k, carry):
        out_total, bias_total = None, None
        for q in range(QZ):
            for inner in range(4):
                z = q * 4 + inner
                grad = jnp.concatenate(
                    [grad_ref[b, k, z : z + 1, :] for b in range(3)] + [jnp.zeros((5, NX), F32)],
                    axis=0,
                )
                upper = grad.astype(BF16)
                lower = (grad - upper.astype(F32)).astype(BF16)
                both = jnp.concatenate([upper, lower], axis=0)
                grad_hidden = dot(out_w_ref[...], both)
                stage[inner * C : inner * C + C, q * NX : q * NX + NX] = (
                    grad_hidden * slope_ref[k, z].astype(F32)
                ).astype(BF16)
                out_term = dot(both, hidden_ref[k, z], NT)
                out_total = out_term if out_total is None else out_total + out_term
            x_rows = dot(table_ref[...], stage[:, q * NX : q * NX + NX], NT)
            put_rows(rows, (step * YB + k) * QZ + q, x_rows)
            bias_total = x_rows[0:8] if bias_total is None else bias_total + x_rows[0:8]
        out_sum[...] += out_total
        bias_sum[...] += bias_total
        cells = jnp.concatenate(
            [cells_ref[k, q * 4 : q * 4 + 4].reshape(4 * C, NX) for q in range(QZ)], axis=1
        )
        point_sum[...] += dot(cells, stage[...], NT)
        return carry

    lax.fori_loop(0, YB, plane, 0)

    @pl.when(step == LY // YB - 1)
    def _():
        emit_rows(rows, rows_ref, odd_ref)
        total = point_sum[0:C, 0:C]
        bias = bias_sum[0:1, 0:C]
        for inner in range(1, 4):
            span = slice(inner * C, inner * C + C)
            total = total + point_sum[span, span]
            bias = bias + bias_sum[0:1, span]
        small_ref[...] = jnp.zeros_like(small_ref)
        small_ref[0:C, 0:C] = total
        small_ref[64:65, 0:C] = bias
        small_ref[72:80, 0:C] = out_sum[0:8] + out_sum[8:16]
        small_ref[80:88, :] = loss_ref[:, 0:128] + loss_ref[:, 128:256]


def grad_dense(hidden, slope, cells, grad_b, out_weight, loss_rows):
    forward = const(tables()[0])
    out_w = jnp.pad(out_weight, ((0, 0), (0, 5)))
    out_w = jnp.concatenate([out_w, out_w], axis=1)
    cell_spec = pl.BlockSpec((YB, LZ, C, NX), lambda y: (y, 0, 0, 0))
    return pl.pallas_call(
        grad_kernel,
        grid=(LY // YB,),
        in_specs=[
            cell_spec,
            cell_spec,
            cell_spec,
            pl.BlockSpec((3, YB, LZ, NX), lambda y: (0, y, 0, 0)),
            whole((40, NX)),
            whole((C, 16)),
            whole((8, NX)),
        ],
        out_specs=[
            whole((GY, 2, 64, NX)),
            whole((64, NX)),
            whole((128, 128)),
        ],
        out_shape=[
            jax.ShapeDtypeStruct((GY, 2, 64, NX), BF16),
            jax.ShapeDtypeStruct((64, NX), BF16),
            jax.ShapeDtypeStruct((128, 128), F32),
        ],
        scratch_shapes=[
            pltpu.VMEM((4 * C, QZ * NX), BF16),
            pltpu.VMEM((2, 40 * 64, 128), F32),
            pltpu.VMEM((4 * C, 4 * C), F32),
            pltpu.VMEM((8, NX), F32),
            pltpu.VMEM((16, C), F32),
        ],
        compiler_params=params(),
        name="grad_dense",
    )(hidden, slope, cells, grad_b, forward, out_w, loss_rows)


DIRECTIONS = [(dy, dz) for dy in (-1, 0, 1) for dz in (-1, 0, 1) if dy or dz]


def halo_kernel(
    field, low, high, corner, y_low, y_high, z_low, z_high, corner_out, send, recv
):
    g, h = lax.axis_index("gy"), lax.axis_index("gz")

    def piece(dy, dz):
        if dz == 0:
            start = LY - 2 if dy > 0 else 0
            return field.at[:, pl.ds(start, 2)], (y_low if dy > 0 else y_high)
        if dy == 0:
            return (high, z_low) if dz > 0 else (low, z_high)
        index = (2 if dy > 0 else 0) + (1 if dz > 0 else 0)
        return corner.at[index], corner_out.at[3 - index]

    def exists(dy, dz):
        y, z = g + dy, h + dz
        return jnp.logical_and(
            jnp.logical_and(y >= 0, y < GY), jnp.logical_and(z >= 0, z < GZ)
        )

    def copy(index):
        dy, dz = DIRECTIONS[index]
        src, dst = piece(dy, dz)
        return pltpu.make_async_remote_copy(
            src_ref=src, dst_ref=dst, send_sem=send.at[index], recv_sem=recv.at[index],
            device_id={"gy": g + dy, "gz": h + dz}, device_id_type=MESH,
        )

    barrier = pltpu.get_barrier_semaphore()
    for dy, dz in DIRECTIONS:

        @pl.when(exists(dy, dz))
        def _(dy=dy, dz=dz):
            pl.semaphore_signal(
                barrier, inc=1, device_id={"gy": g + dy, "gz": h + dz}, device_id_type=MESH
            )

    y_sides = jnp.where(g > 0, 1, 0) + jnp.where(g < GY - 1, 1, 0)
    z_sides = jnp.where(h > 0, 1, 0) + jnp.where(h < GZ - 1, 1, 0)
    pl.semaphore_wait(barrier, (y_sides + 1) * (z_sides + 1) - 1)
    for index in range(8):

        @pl.when(exists(*DIRECTIONS[index]))
        def _(index=index):
            copy(index).start()

    for index in range(8):
        dy, dz = DIRECTIONS[index]

        @pl.when(exists(dy, dz))
        def _(index=index):
            copy(index).wait_send()

        @pl.when(exists(-dy, -dz))
        def _(index=index):
            copy(index).wait_recv()


def halo(collective_id, field, low, high, corner):
    side = jax.ShapeDtypeStruct((3, 2, LZ, NX), F32)
    edge = jax.ShapeDtypeStruct((3, 32, NX), F32)
    return pl.pallas_call(
        halo_kernel,
        out_shape=[side, side, edge, edge, jax.ShapeDtypeStruct((4, 8, NX), F32)],
        in_specs=[ANY] * 4,
        out_specs=[ANY] * 5,
        scratch_shapes=[pltpu.SemaphoreType.DMA((8,))] * 2,
        compiler_params=pltpu.CompilerParams(
            collective_id=collective_id, has_side_effects=True
        ),
        name="halo",
    )(field, low, high, corner)


def cell_loss(field_b, slope_x, slope_y, slope_z):
    current_x = slope_y[2] - slope_z[1]
    current_y = slope_z[0] - slope_x[2]
    current_z = slope_x[1] - slope_y[0]
    force_x = current_y * field_b[2] - current_z * field_b[1]
    force_y = current_z * field_b[0] - current_x * field_b[2]
    force_z = current_x * field_b[1] - current_y * field_b[0]
    spread = slope_x[0] + slope_y[1] + slope_z[2]
    strength = field_b[0] * field_b[0] + field_b[1] * field_b[1] + field_b[2] * field_b[2] + 1.0
    return (force_x * force_x + force_y * force_y + force_z * force_z) / strength + spread * spread


def stencil_kernel(
    place_ref, field_ref, y_low_ref, y_high_ref, z_low_ref, z_high_ref, corner_ref,
    grad_ref, loss_ref, wide, own, slopes,
):
    g, h = place_ref[0], place_ref[1]
    zero_rows = jnp.zeros((8, NX), F32)

    def kept(present, value):
        return jnp.where(present, value, jnp.zeros_like(value))

    for b in range(3):
        wide[b, 2:18, 8:24, :] = field_ref[b]
        wide[b, 0:2, 8:24, :] = kept(g > 0, y_low_ref[b])
        wide[b, 18:20, 8:24, :] = kept(g < GY - 1, y_high_ref[b])
        for plane in (0, 1, 18, 19):
            wide[b, plane, 0:8, :] = zero_rows
            wide[b, plane, 24:32, :] = zero_rows
        for y in range(LY):
            wide[b, y + 2, 0:8, :] = zero_rows
            wide[b, y + 2, 24:32, :] = zero_rows
            wide[b, y + 2, 6:8, :] = kept(h > 0, z_low_ref[b, 2 * y : 2 * y + 2, :])
            wide[b, y + 2, 24:26, :] = kept(h < GZ - 1, z_high_ref[b, 2 * y : 2 * y + 2, :])
        for index in range(4):
            y_side = g < GY - 1 if index // 2 else g > 0
            z_side = h < GZ - 1 if index % 2 else h > 0
            row = 24 if index % 2 else 7
            wide[b, 18 if index // 2 else 1, row : row + 1, :] = kept(
                jnp.logical_and(y_side, z_side), corner_ref[index, b : b + 1, :]
            )
    lane = lax.broadcasted_iota(jnp.int32, (32, NX), 1)
    row = lax.broadcasted_iota(jnp.int32, (32, NX), 0)
    z_cell = h * LZ + row - 8
    weight = jnp.where((z_cell >= 0) & (z_cell < NZ), 1.0 / CELLS, 0.0).astype(F32)
    inner = (row >= 8) & (row < 24)

    def x_diff(value):
        after = jnp.where(lane == NX - 1, 0.0, pltpu.roll(value, NX - 1, 1))
        before = jnp.where(lane == 0, 0.0, pltpu.roll(value, 1, 1))
        return (after - before) * 0.5

    def z_diff(value):
        return (pltpu.roll(value, 31, 0) - pltpu.roll(value, 1, 0)) * 0.5

    def one(plane, loss):
        cells = tuple(wide[b, plane] for b in range(3))
        slope_x = tuple(x_diff(value) for value in cells)
        slope_y = tuple((wide[b, plane + 1] - wide[b, plane - 1]) * 0.5 for b in range(3))
        slope_z = tuple(z_diff(value) for value in cells)
        terms, pullback = jax.vjp(cell_loss, cells, slope_x, slope_y, slope_z)
        y_cell = g * LY + plane - 2
        y_inside = jnp.logical_and(y_cell >= 0, y_cell < NY)
        grad_own, grad_x, grad_y, grad_z = pullback(jnp.where(y_inside, weight, 0.0))
        for b in range(3):
            own[b, plane - 1] = grad_own[b] - x_diff(grad_x[b]) - z_diff(grad_z[b])
            slopes[b, plane - 1] = grad_y[b]
        counted = jnp.logical_and(plane >= 2, plane < 18)
        return loss + jnp.where(jnp.logical_and(inner, counted), terms, 0.0)

    loss = lax.fori_loop(1, 19, one, jnp.zeros((32, NX), F32))
    total_loss = loss

    def finish(y, sums):
        result = []
        for b in range(3):
            grad = own[b, y + 1, 8:24, :] + (
                slopes[b, y, 8:24, :] - slopes[b, y + 2, 8:24, :]
            ) * 0.5
            grad_ref[b, y] = grad
            result.append(sums[b] + grad)
        return tuple(result)

    sums = lax.fori_loop(0, LY, finish, tuple(jnp.zeros((LZ, NX), F32) for _ in range(3)))
    loss_ref[...] = jnp.zeros_like(loss_ref)
    for index, value in enumerate((total_loss,) + sums):
        loss_ref[index : index + 1, :] = jnp.sum(value, axis=0, keepdims=True)


def stencil(place, field, *halos):
    vmem = pl.BlockSpec(memory_space=pltpu.VMEM)
    return pl.pallas_call(
        stencil_kernel,
        in_specs=[pl.BlockSpec(memory_space=pltpu.SMEM)] + [vmem] * 6,
        out_specs=[vmem] * 2,
        out_shape=[
            jax.ShapeDtypeStruct((3, LY, LZ, NX), F32),
            jax.ShapeDtypeStruct((8, NX), F32),
        ],
        scratch_shapes=[
            pltpu.VMEM((3, 20, 32, NX), F32),
            pltpu.VMEM((3, 18, 32, NX), F32),
            pltpu.VMEM((3, 18, 32, NX), F32),
        ],
        compiler_params=params(),
        name="stencil",
    )(place, field, *halos)


def on_device(field_in, spectral_weight, point_weight, point_bias, out_weight, out_bias):
    place = jnp.stack([lax.axis_index("gy"), lax.axis_index("gz")]).astype(jnp.int32)
    cells, rows, odd = x_transform(field_in)
    rows, odd = swap("gy", GY, 1, ("swap", rows), ("to0", odd))
    modes_in = to_kx(to_modes(2, SCALE, rows, odd).astype(BF16))

    mixed = jnp.einsum(
        "abkpi,abkio->abkpo", modes_in, spectral_weight, preferred_element_type=F32
    )
    real = mixed[..., 0, :C] - mixed[..., 1, C:]
    imag = mixed[..., 0, C:] + mixed[..., 1, :C]
    modes_out = jnp.stack([real, imag], axis=3)

    rows, odd = from_modes(4, from_kx(modes_out))
    rows, odd = swap("gy", GY, 6, ("swap", rows), ("from0", odd))

    hidden, slope, field_b, *edges = dense(
        rows, odd, cells, point_weight, point_bias, out_weight, out_bias
    )
    grad_b, loss_rows = stencil(place, field_b, *halo(10, field_b, *edges))
    rows, odd, small = grad_dense(hidden, slope, cells, grad_b, out_weight, loss_rows)
    small = small.reshape(GY, 8, 128)
    rows, odd, small = swap("gy", GY, 7, ("swap", rows), ("to0", odd), ("swap", small))
    dealt, small = to_modes(8, 1.0, rows, odd, small)
    small = small.reshape(128, 128)
    grad_modes = to_kx(dealt.astype(BF16))
    grad_spectral = weight_grad(modes_in, grad_modes).reshape(4, 2, M, C, 2 * C)
    scalars = jnp.sum(small[80:84], axis=1)
    return (
        scalars[0] / CELLS,
        grad_spectral,
        small[:C, :C],
        small[64, :C],
        small[72:75, :C].T,
        scalars[1:4],
    )


def solution(mesh):
    return jax.shard_map(
        on_device,
        mesh=mesh,
        in_specs=(P(None, "gy", "gz", None), P("gz", "gy", None, None, None), P(), P(), P(), P()),
        out_specs=(P(), P("gz", "gy", None, None, None), P(), P(), P(), P()),
        check_vma=False,
    )
```

```python
import functools
import math

import jax
import jax.numpy as jnp
import numpy as np
from jax import lax
from jax.experimental import pallas as pl
from jax.experimental.pallas import tpu as pltpu
from jax.sharding import PartitionSpec as P

NX, NY, NZ = 256, 256, 128
M = 32
C = 64
GY, GZ = 16, 8
LY, LZ = 16, 16
YB = 2
QZ = 4
F32, BF16 = jnp.float32, jnp.bfloat16
SCALE = math.sqrt(M * M * M / (NX * NY * NZ))
CELLS = NX * NY * NZ
DENSITY = 1.0 / math.sqrt(math.pi)
MESH = pl.DeviceIdType.MESH
ANY = pl.BlockSpec(memory_space=pl.ANY)
NEAR = pl.BlockSpec(memory_space=pltpu.VMEM)
FAR = pl.BlockSpec(memory_space=pltpu.HBM)


def np_table(length):
    mode = np.arange(M)
    wave = np.where(mode < M // 2, mode, mode - M)
    product = (np.arange(length)[:, None] * wave[None, :]) % length
    phases = product.astype(np.float64) * (2.0 * math.pi / length)
    return np.cos(phases), np.sin(phases)


@functools.lru_cache(None)
def tables():
    cos_x, sin_x = np_table(NX)
    forward = np.zeros((40, NX))
    forward[:16] = cos_x[:, :16].T
    forward[16] = cos_x[:, 16]
    forward[17:32] = sin_x[:, 1:16].T
    forward[32] = sin_x[:, 16]
    inverse = np.zeros((40, NX))
    inverse[33:36] = 1.0
    inverse[0:32:2] = forward[:16]
    inverse[1:32:2] = forward[16:32]
    inverse[32] = forward[32]
    cos_y, sin_y = np_table(NY)
    y_rows = np.kron(np.concatenate([cos_y, sin_y], axis=1).T, np.eye(QZ))
    cos_z, sin_z = np_table(NZ)
    z_rows = []
    for table in (cos_z, sin_z):
        cells = table.reshape(GZ, QZ, 4, M)
        for inner in range(4):
            part = cells[:, :, inner, :].reshape(GZ, QZ, GZ, 4)
            full = np.zeros((GZ, 2, 4, 2, GZ, 4, QZ))
            for gs in range(2):
                for ky2 in range(2):
                    full[:, gs, :, ky2, :, gs * 2 + ky2, :] = part.transpose(2, 3, 0, 1)
            z_rows.append(full.reshape(128, 128))
    z_rows = np.stack(z_rows).reshape(2, 4, 128, 128)
    return forward, inverse, y_rows, z_rows


def const(value):
    return jnp.asarray(value, BF16)


NT = (((1,), (1,)), ((), ()))
TN = (((0,), (0,)), ((), ()))


def dot(left, right, dims=(((1,), (0,)), ((), ()))):
    return lax.dot_general(left, right, dims, preferred_element_type=F32)


def whole(shape):
    return pl.BlockSpec(shape, lambda *_: (0,) * len(shape))


def params(limit=56 << 20):
    return pltpu.CompilerParams(vmem_limit_bytes=limit)


def swap_kernel(axis, count, modes, *refs):
    size = len(modes)
    srcs, dsts, sends, recvs = [refs[i * size : i * size + size] for i in range(4)]
    local = refs[4 * size]
    me = lax.axis_index(axis)
    barrier = pltpu.get_barrier_semaphore()
    for step in range(1, count):
        pl.semaphore_signal(
            barrier, inc=1, device_id={axis: (me + step) % count}, device_id_type=MESH
        )
    pl.semaphore_wait(barrier, count - 1)

    def remote(src, dst, send, recv, peer):
        return pltpu.make_async_remote_copy(
            src_ref=src, dst_ref=dst, send_sem=send, recv_sem=recv,
            device_id={axis: peer}, device_id_type=MESH,
        )

    copies, early, late = [], [], []
    for index, mode in enumerate(modes):
        src, dst, send, recv = srcs[index], dsts[index], sends[index], recvs[index]
        if mode == "to0":

            def begin(step, src=src, dst=dst, send=send, recv=recv):
                @pl.when(jnp.logical_and(me != 0, me == step))
                def _():
                    remote(src, dst.at[me], send.at[0], recv.at[me], 0).start()

            early.append(begin)

            @pl.when(me == 0)
            def _(src=src, dst=dst, index=index):
                pltpu.make_async_copy(src, dst.at[0], local.at[index]).start()

            def finish(src=src, dst=dst, send=send, recv=recv, index=index):
                @pl.when(me != 0)
                def _():
                    remote(src, dst.at[me], send.at[0], recv.at[me], 0).wait_send()

                @pl.when(me == 0)
                def _():
                    pltpu.make_async_copy(src, dst.at[0], local.at[index]).wait()
                    for k in range(1, count):
                        remote(src, dst.at[k], send.at[0], recv.at[k], k).wait_recv()

            late.append(finish)
        elif mode == "from0":

            @pl.when(me == 0)
            def _(src=src, dst=dst, send=send, recv=recv, index=index):
                pltpu.make_async_copy(src.at[0], dst, local.at[index]).start()
                for k in range(1, count):
                    remote(src.at[k], dst, send.at[k], recv.at[0], k).start()

            def finish(src=src, dst=dst, send=send, recv=recv, index=index):
                @pl.when(me == 0)
                def _():
                    pltpu.make_async_copy(src.at[0], dst, local.at[index]).wait()
                    for k in range(1, count):
                        remote(src.at[k], dst, send.at[k], recv.at[0], k).wait_send()

                @pl.when(me != 0)
                def _():
                    remote(src.at[0], dst, send.at[0], recv.at[0], 0).wait_recv()

            late.append(finish)
        else:
            piece = (lambda p, src=src: src.at[p]) if mode == "swap" else (lambda p, src=src: src)
            copies.append((0, pltpu.make_async_copy(piece(me), dst.at[me], local.at[index])))
            for step in range(1, count):
                peer = (me + step) % count
                copies.append(
                    (step, remote(piece(peer), dst.at[me], send.at[step], recv.at[step], peer))
                )
    for step in range(count):
        for at, copy in copies:
            if at == step:
                copy.start()
        for begin in early:
            begin(step)
    copies = [copy for _, copy in copies]
    for copy in copies:
        copy.wait()
    for finish in late:
        finish()


def swap(axis, count, collective_id, spaces, *operands):
    modes = tuple(mode for mode, _ in operands)
    args = [value for _, value in operands]
    outs = []
    for mode, value in operands:
        shape = value.shape
        if mode in ("all", "to0"):
            shape = (count,) + shape
        elif mode == "from0":
            shape = shape[1:]
        outs.append(jax.ShapeDtypeStruct(shape, value.dtype))
    size = len(args)
    result = pl.pallas_call(
        functools.partial(swap_kernel, axis, count, modes),
        out_shape=outs,
        in_specs=[spaces[0]] * size,
        out_specs=[spaces[1]] * size,
        scratch_shapes=[pltpu.SemaphoreType.DMA((count,))] * (2 * size)
        + [pltpu.SemaphoreType.DMA((size,))],
        compiler_params=pltpu.CompilerParams(
            collective_id=collective_id, has_side_effects=True, vmem_limit_bytes=16 << 20
        ),
        name=f"swap_{collective_id}",
    )(*args)
    return result if size > 1 else result[0]


def emit_rows(rows_ref, out_ref, extra_ref):
    for half in range(2):
        lanes = slice(half * 128, half * 128 + 128)
        for g in range(GY):
            for part in range(2):
                start = (part * GY + g) * 64
                out_ref[g, part, :, lanes] = rows_ref[half, start : start + 64, :].astype(BF16)
        extra_ref[:, lanes] = rows_ref[half, 2048:2112, :].astype(BF16)


def put_rows(rows_ref, start, value):
    for half in range(2):
        rows_ref[half, pl.ds(start, 40, stride=64), :] = value[:, half * 128 : half * 128 + 128]


def x_kernel(field_ref, table_ref, cells_ref, out_ref, extra_ref, stage, rows):
    step = pl.program_id(0)

    def plane(k, carry):
        for half in range(2):
            lanes = slice(half * 128, half * 128 + 128)
            stage[half] = field_ref[:, k, :, lanes].astype(F32).reshape(C * LZ, 128)
            for z in range(LZ):
                cells_ref[k, z, :, lanes] = stage[half, pl.ds(z, C, stride=LZ), :].astype(BF16)
        for q in range(QZ):
            block = cells_ref[k, q * 4 : q * 4 + 4].reshape(4 * C, NX)
            put_rows(rows, (step * YB + k) * QZ + q, dot(table_ref[...], block, NT))
        return carry

    lax.fori_loop(0, YB, plane, 0)

    @pl.when(step == LY // YB - 1)
    def _():
        emit_rows(rows, out_ref, extra_ref)


def x_transform(field_in):
    forward = const(tables()[0])
    return pl.pallas_call(
        x_kernel,
        grid=(LY // YB,),
        in_specs=[
            pl.BlockSpec((C, YB, LZ, NX), lambda y: (0, y, 0, 0)),
            whole((40, NX)),
        ],
        out_specs=[
            pl.BlockSpec((YB, LZ, C, NX), lambda y: (y, 0, 0, 0)),
            whole((GY, 2, 64, NX)),
            whole((64, NX)),
        ],
        out_shape=[
            jax.ShapeDtypeStruct((LY, LZ, C, NX), BF16),
            jax.ShapeDtypeStruct((GY, 2, 64, NX), BF16),
            jax.ShapeDtypeStruct((64, NX), BF16),
        ],
        scratch_shapes=[pltpu.VMEM((2, C * LZ, 128), F32), pltpu.VMEM((2, 40 * 64, 128), F32)],
        compiler_params=params(),
        name="x_transform",
    )(field_in, forward)


def y_body(first, src_ref, extra_ref, table_ref, out_ref):
    sums = []
    for part in range(2):
        sums.append(dot(table_ref[...], src_ref[:, part].reshape(GY * 64, NX)))
    sums.append(dot(table_ref[...], extra_ref[...].reshape(GY * 64, NX)))
    zero = jnp.zeros((128, NX), F32)
    cc, cs = sums[0][:128], sums[0][128:]
    sc, ss = sums[1][:128], sums[1][128:]
    ec, es = sums[2][:128], sums[2][128:]
    pc, ps = jnp.where(first, zero, sc), jnp.where(first, zero, ss)
    nc, ns = jnp.where(first, sc, cc), jnp.where(first, ss, cs)
    mc, ms = jnp.where(first, ec, -sc), jnp.where(first, es, -ss)
    parts = (cc - ps, -(cs + pc), nc - ms, -(ns + mc))
    for index, part in enumerate(parts):
        out_ref[:, index] = part.astype(BF16).reshape(GZ, 16, NX)


def y_back_body(first, src_ref, table_ref, out_ref, extra_ref):
    ar, ai, br, bi = [
        src_ref[:, part].reshape(128, NX).astype(F32) for part in range(4)
    ]
    rows = (
        (jnp.where(first, ar, ar + br), jnp.where(first, -ai, -(ai + bi))),
        (jnp.where(first, br, bi - ai), jnp.where(first, -bi, br - ar)),
        (jnp.where(first, -bi, 0.0), jnp.where(first, -br, 0.0)),
    )
    for part, (upper, lower) in enumerate(rows):
        operand = jnp.concatenate([upper, lower], axis=0).astype(BF16)
        result = dot(table_ref[...], operand).astype(BF16).reshape(GY, 64, NX)
        if part < 2:
            out_ref[:, part] = result
        else:
            extra_ref[...] = result


def z_body(factor, src_ref, table_ref, out_ref):
    for m in range(2):
        sums = []
        for p in range(2):
            block = src_ref[:, m * 2 + p].reshape(128, NX)
            pair = []
            for t in range(2):
                total = None
                for inner in range(4):
                    term = dot(table_ref[t, inner], block[:, inner * C : inner * C + C])
                    total = term if total is None else total + term
                pair.append(total)
            sums.append(pair)
        real = sums[0][0] + sums[1][1]
        imag = sums[1][0] - sums[0][1]
        out_ref[:, :, m * 128 : m * 128 + 128] = (
            jnp.concatenate([real, imag], axis=1) * factor
        ).reshape(GY, 8, 128)


def z_back_body(src_ref, table_ref, out_ref):
    for m in range(2):
        block = src_ref[:, :, m * 128 : m * 128 + 128].reshape(128, 128).astype(BF16)
        real, imag = [], []
        for inner in range(4):
            cos_part = dot(table_ref[0, inner], block)
            sin_part = dot(table_ref[1, inner], block)
            real.append(cos_part[:, :C] - sin_part[:, C:])
            imag.append(cos_part[:, C:] + sin_part[:, :C])
        for p, pieces in enumerate((real, imag)):
            full = jnp.concatenate(pieces, axis=1).astype(BF16)
            out_ref[:, m * 2 + p] = full.reshape(GZ, 16, NX)


def mode_places():
    g, h = lax.axis_index("gy"), lax.axis_index("gz")
    owners = [(2 * h + j % 2, j // 2) for j in range(GY)]
    holders = [(k, g // 2) for k in range(GY)]
    return g, h, owners, holders


def greet(g, h, sources, with_gy):
    barrier = pltpu.get_barrier_semaphore()
    for step in range(1, GZ):
        pl.semaphore_signal(
            barrier, inc=1, device_id={"gz": (h + step) % GZ}, device_id_type=MESH
        )
    if with_gy:
        for step in range(1, GY):
            pl.semaphore_signal(
                barrier, inc=1, device_id={"gy": (g + step) % GY}, device_id_type=MESH
            )
    for y, z in sources:

        @pl.when(jnp.logical_not(jnp.logical_and(y == g, z == h)))
        def _(y=y, z=z):
            pl.semaphore_signal(barrier, inc=1, device_id={"gy": y, "gz": z}, device_id_type=MESH)


def await_greetings(g, h, with_gy):
    fixed = GZ - 1 + (GY - 1 if with_gy else 0)
    pl.semaphore_wait(
        pltpu.get_barrier_semaphore(), jnp.where(g // 2 == h, GY - 1, GY) + fixed
    )


def spread(axis, count, me, piece, dst, send, recv, local):
    copies = [pltpu.make_async_copy(piece(me), dst.at[me], local)]
    for step in range(1, count):
        peer = (me + step) % count
        copies.append(
            pltpu.make_async_remote_copy(
                src_ref=piece(peer), dst_ref=dst.at[me],
                send_sem=send.at[step], recv_sem=recv.at[step],
                device_id={axis: peer}, device_id_type=MESH,
            )
        )
    for copy in copies:
        copy.start()
    return copies


def deal(g, h, targets, sources, slot, src, dst, send, recv, local):
    def is_me(device):
        return jnp.logical_and(device[0] == g, device[1] == h)

    def remote(j, device, landing, arrived):
        return pltpu.make_async_remote_copy(
            src_ref=src.at[j], dst_ref=dst.at[landing],
            send_sem=send.at[j], recv_sem=recv.at[arrived],
            device_id={"gy": device[0], "gz": device[1]}, device_id_type=MESH,
        )

    for j in range(GY):
        mine = is_me(targets[j])

        @pl.when(jnp.logical_not(mine))
        def _(j=j):
            remote(j, targets[j], slot, slot).start()

        @pl.when(mine)
        def _(j=j):
            copy = pltpu.make_async_copy(src.at[j], dst.at[slot], local)
            copy.start()
            copy.wait()

    for j in range(GY):

        @pl.when(jnp.logical_not(is_me(targets[j])))
        def _(j=j):
            remote(j, targets[j], slot, slot).wait_send()

        @pl.when(jnp.logical_not(is_me(sources[j])))
        def _(j=j):
            remote(j, sources[j], j, j).wait_recv()


def to_modes_kernel(factor, with_small, *refs):
    if with_small:
        (rows, extra, y_table, z_table, small, dealt, small_out, y_out, z_in, z_out,
         send, recv, send2, recv2, local, small_a, small_b, small_c,
         send3, recv3, send4, recv4) = refs
    else:
        (rows, extra, y_table, z_table, dealt, y_out, z_in, z_out,
         send, recv, send2, recv2, local) = refs
    g, h, owners, holders = mode_places()
    greet(g, h, holders, with_small)
    y_body(g == 0, rows, extra, y_table, y_out)
    if with_small:
        small_a[...] = jnp.sum(small[...], axis=0)
    await_greetings(g, h, with_small)
    copies = spread("gz", GZ, h, lambda p: y_out.at[p], z_in, send, recv, local.at[0])
    if with_small:
        copies += spread("gz", GZ, h, lambda p: small_a, small_b, send3, recv3, local.at[1])
    for copy in copies:
        copy.wait()
    z_body(factor, z_in, z_table, z_out)
    copies = []
    if with_small:
        small_c[...] = jnp.sum(small_b[...], axis=0)
        copies = spread("gy", GY, g, lambda p: small_c, small_out, send4, recv4, local.at[2])
    deal(g, h, owners, holders, g, z_out, dealt, send2, recv2, local.at[3])
    for copy in copies:
        copy.wait()


def to_modes(collective_id, factor, rows, extra, small=None):
    vmem = pl.BlockSpec(memory_space=pltpu.VMEM)
    args = [rows, extra, const(tables()[2]), const(tables()[3])]
    outs = [jax.ShapeDtypeStruct((GY, 8, 256), F32)]
    block = pltpu.VMEM((GZ, 4, 16, NX), BF16)
    gz_sems = [pltpu.SemaphoreType.DMA((GZ,))] * 2
    gy_sems = [pltpu.SemaphoreType.DMA((GY,))] * 2
    scratch = [block, block, pltpu.VMEM((GY, 8, 256), F32)]
    scratch += gz_sems + gy_sems + [pltpu.SemaphoreType.DMA((4,))]
    if small is not None:
        args.append(small)
        outs.append(jax.ShapeDtypeStruct((GY, 8, 128), F32))
        scratch += [
            pltpu.VMEM((8, 128), F32),
            pltpu.VMEM((GZ, 8, 128), F32),
            pltpu.VMEM((8, 128), F32),
        ]
        scratch += gz_sems + gy_sems
    result = pl.pallas_call(
        functools.partial(to_modes_kernel, factor, small is not None),
        out_shape=outs,
        in_specs=[vmem] * len(args),
        out_specs=[ANY] * len(outs),
        scratch_shapes=scratch,
        compiler_params=pltpu.CompilerParams(
            collective_id=collective_id, has_side_effects=True, vmem_limit_bytes=40 << 20
        ),
        name=f"to_modes_{collective_id}",
    )(*args)
    return result if small is not None else result[0]


def from_modes_kernel(
    modes, y_table, z_table, rows, extra, landed, z_out, y_in, send, recv, send2, recv2, local
):
    g, h, owners, holders = mode_places()
    greet(g, h, owners, False)
    await_greetings(g, h, False)
    deal(g, h, holders, owners, h * 2 + g % 2, modes, landed, send2, recv2, local.at[1])
    z_back_body(landed, z_table, z_out)
    copies = spread("gz", GZ, h, lambda p: z_out.at[p], y_in, send, recv, local.at[0])
    for copy in copies:
        copy.wait()
    y_back_body(g == 0, y_in, y_table, rows, extra)


def from_modes(collective_id, modes):
    vmem = pl.BlockSpec(memory_space=pltpu.VMEM)
    block = pltpu.VMEM((GZ, 4, 16, NX), BF16)
    return pl.pallas_call(
        from_modes_kernel,
        out_shape=[
            jax.ShapeDtypeStruct((GY, 2, 64, NX), BF16),
            jax.ShapeDtypeStruct((GY, 64, NX), BF16),
        ],
        in_specs=[vmem] * 3,
        out_specs=[vmem] * 2,
        scratch_shapes=[pltpu.VMEM((GY, 8, 256), F32), block, block]
        + [pltpu.SemaphoreType.DMA((GZ,))] * 2
        + [pltpu.SemaphoreType.DMA((GY,))] * 2
        + [pltpu.SemaphoreType.DMA((2,))],
        compiler_params=pltpu.CompilerParams(
            collective_id=collective_id, has_side_effects=True, vmem_limit_bytes=40 << 20
        ),
        name=f"from_modes_{collective_id}",
    )(modes, const(tables()[2].T), const(tables()[3].transpose(0, 1, 3, 2)))


def to_kx(dealt):
    split = dealt.reshape(GY, 4, 2, 2, 2, C)
    plus, minus = split[:, :, :, 0], split[:, :, :, 1]
    order = jnp.concatenate([plus, minus[:1], minus[1:][::-1]], axis=0)
    return order.transpose(1, 2, 0, 3, 4)


def from_kx(modes):
    order = modes.transpose(2, 0, 1, 3, 4)
    minus = jnp.concatenate([order[16:17], order[17:][::-1]], axis=0)
    return jnp.stack([order[:16], minus], axis=3).reshape(GY, 8, 256)


def weight_grad_kernel(u_ref, g_ref, mask_ref, out_ref):
    for block in range(4):
        right = jnp.concatenate([g_ref[block]] * 8, axis=1) * mask_ref[...]
        result = dot(u_ref[block], right, TN)
        for mode in range(8):
            out_ref[0, block * 8 + mode] = result[:, mode * 128 : mode * 128 + 128]


def weight_grad(modes_in, grad_modes):
    u = modes_in.reshape(M, 16, C)
    real, imag = grad_modes[..., 0, :], grad_modes[..., 1, :]
    g = jnp.stack(
        [jnp.concatenate([real, imag], axis=-1), jnp.concatenate([imag, -real], axis=-1)], axis=3
    ).reshape(M, 16, 128)
    mask = const(np.kron(np.eye(8), np.ones((2, 128))))
    return pl.pallas_call(
        weight_grad_kernel,
        grid=(8,),
        in_specs=[
            pl.BlockSpec((4, 16, C), lambda i: (i, 0, 0)),
            pl.BlockSpec((4, 16, 128), lambda i: (i, 0, 0)),
            whole((16, 1024)),
        ],
        out_specs=pl.BlockSpec((1, M, C, 128), lambda i: (i, 0, 0, 0)),
        out_shape=jax.ShapeDtypeStruct((8, M, C, 128), F32),
        compiler_params=params(),
        name="weight_grad",
    )(u, g, mask)


def dense_kernel(
    rows_ref, odd_ref, cells_ref, table_ref, point_ref, bias_ref, out_w_ref, out_b_ref,
    hidden_ref, slope_ref, field_ref, low_ref, high_ref, corner_ref, rows,
):
    step = pl.program_id(0)

    @pl.when(step == 0)
    def _():
        corner_ref[...] = jnp.zeros_like(corner_ref)
        for half in range(2):
            lanes = slice(half * 128, half * 128 + 128)
            for g in range(GY * 2):
                rows[half, g * 64 : g * 64 + 64, :] = rows_ref[g, :, lanes].astype(F32)
            rows[half, 2048:2112, :] = odd_ref[:, lanes].astype(F32)
            rest = bias_ref[...]
            for part in range(3):
                piece = rest.astype(BF16).astype(F32)
                start = 2112 + part * 64
                rows[half, start : start + 64, :] = jnp.broadcast_to(piece, (64, 128))
                rest = rest - piece
            rows[half, 2304:2560, :] = jnp.zeros((256, 128), F32)

    def plane(k, carry):
        y = step * YB + k
        for q in range(QZ):
            picked = jnp.concatenate(
                [rows[half, pl.ds(y * QZ + q, 40, stride=64), :] for half in range(2)], axis=1
            ).astype(BF16)
            spectral = dot(picked, table_ref[...], TN)
            for inner in range(4):
                z = q * 4 + inner
                pre = spectral[inner * C : inner * C + C] + dot(point_ref[...], cells_ref[k, z])
                scaled = pre * math.sqrt(0.5)
                normal_cdf = 0.5 * lax.erf(scaled) + 0.5
                decay = jnp.exp2(scaled * scaled * -math.log2(math.e))
                hidden = (pre * normal_cdf).astype(BF16)
                hidden_ref[k, z] = hidden
                slope_ref[k, z] = (normal_cdf + scaled * DENSITY * decay).astype(BF16)
                b_rows = dot(out_w_ref[...], hidden)
                for b in range(3):
                    field_ref[b, k, z : z + 1, :] = b_rows[b : b + 1] + out_b_ref[b]
        for b in range(3):
            for i in range(2):
                z = LZ - 2 + i
                low_ref[b, pl.ds(y * 2 + i, 1), :] = field_ref[b, k, i : i + 1, :]
                high_ref[b, pl.ds(y * 2 + i, 1), :] = field_ref[b, k, z : z + 1, :]
        return carry

    lax.fori_loop(0, YB, plane, 0)
    for y_edge in range(2):

        @pl.when(step == y_edge * (LY // YB - 1))
        def _(y_edge=y_edge):
            for b in range(3):
                for z_edge in range(2):
                    z = z_edge * (LZ - 1)
                    corner_ref[y_edge * 2 + z_edge, b : b + 1, :] = field_ref[
                        b, y_edge * (YB - 1), z : z + 1, :
                    ]


def dense(rows, odd, cells, point_weight, point_bias, out_weight, out_bias):
    out_w = jnp.pad(out_weight.T, ((0, 5), (0, 0)))
    cell_spec = pl.BlockSpec((YB, LZ, C, NX), lambda y: (y, 0, 0, 0))
    cell_shape = jax.ShapeDtypeStruct((LY, LZ, C, NX), BF16)
    return pl.pallas_call(
        dense_kernel,
        grid=(LY // YB,),
        in_specs=[
            whole((GY * 2, 64, NX)),
            whole((64, NX)),
            cell_spec,
            whole((40, NX)),
            whole((C, C)),
            whole((1, 128)),
            whole((8, C)),
            pl.BlockSpec(memory_space=pltpu.SMEM),
        ],
        out_specs=[
            cell_spec,
            cell_spec,
            pl.BlockSpec((3, YB, LZ, NX), lambda y: (0, y, 0, 0)),
            whole((3, 32, NX)),
            whole((3, 32, NX)),
            whole((4, 8, NX)),
        ],
        out_shape=[
            cell_shape,
            cell_shape,
            jax.ShapeDtypeStruct((3, LY, LZ, NX), F32),
            jax.ShapeDtypeStruct((3, 32, NX), F32),
            jax.ShapeDtypeStruct((3, 32, NX), F32),
            jax.ShapeDtypeStruct((4, 8, NX), F32),
        ],
        scratch_shapes=[pltpu.VMEM((2, 40 * 64, 128), F32)],
        compiler_params=params(),
        name="dense",
    )(
        rows.reshape(GY * 2, 64, NX),
        odd,
        cells,
        const(tables()[1]),
        point_weight.T,
        jnp.concatenate([point_bias, point_bias])[None],
        out_w,
        out_bias,
    )


def grad_kernel(
    hidden_ref, slope_ref, cells_ref, grad_ref, table_ref, out_w_ref, loss_ref,
    rows_ref, odd_ref, small_ref,
    stage, rows, point_sum, bias_sum, out_sum,
):
    step = pl.program_id(0)

    @pl.when(step == 0)
    def _():
        point_sum[...] = jnp.zeros_like(point_sum)
        bias_sum[...] = jnp.zeros_like(bias_sum)
        out_sum[...] = jnp.zeros_like(out_sum)

    def plane(k, carry):
        out_total, bias_total = None, None
        for q in range(QZ):
            for inner in range(4):
                z = q * 4 + inner
                grad = jnp.concatenate(
                    [grad_ref[b, k, z : z + 1, :] for b in range(3)] + [jnp.zeros((5, NX), F32)],
                    axis=0,
                )
                upper = grad.astype(BF16)
                lower = (grad - upper.astype(F32)).astype(BF16)
                both = jnp.concatenate([upper, lower], axis=0)
                grad_hidden = dot(out_w_ref[...], both)
                stage[inner * C : inner * C + C, q * NX : q * NX + NX] = (
                    grad_hidden * slope_ref[k, z].astype(F32)
                ).astype(BF16)
                out_term = dot(both, hidden_ref[k, z], NT)
                out_total = out_term if out_total is None else out_total + out_term
            x_rows = dot(table_ref[...], stage[:, q * NX : q * NX + NX], NT)
            put_rows(rows, (step * YB + k) * QZ + q, x_rows)
            bias_total = x_rows[0:8] if bias_total is None else bias_total + x_rows[0:8]
        out_sum[...] += out_total
        bias_sum[...] += bias_total
        cells = jnp.concatenate(
            [cells_ref[k, q * 4 : q * 4 + 4].reshape(4 * C, NX) for q in range(QZ)], axis=1
        )
        point_sum[...] += dot(cells, stage[...], NT)
        return carry

    lax.fori_loop(0, YB, plane, 0)

    @pl.when(step == LY // YB - 1)
    def _():
        emit_rows(rows, rows_ref, odd_ref)
        total = point_sum[0:C, 0:C]
        bias = bias_sum[0:1, 0:C]
        for inner in range(1, 4):
            span = slice(inner * C, inner * C + C)
            total = total + point_sum[span, span]
            bias = bias + bias_sum[0:1, span]
        small_ref[...] = jnp.zeros_like(small_ref)
        small_ref[0:C, 0:C] = total
        small_ref[64:65, 0:C] = bias
        small_ref[72:80, 0:C] = out_sum[0:8] + out_sum[8:16]
        small_ref[80:88, :] = loss_ref[:, 0:128] + loss_ref[:, 128:256]


def grad_dense(hidden, slope, cells, grad_b, out_weight, loss_rows):
    forward = const(tables()[0])
    out_w = jnp.pad(out_weight, ((0, 0), (0, 5)))
    out_w = jnp.concatenate([out_w, out_w], axis=1)
    cell_spec = pl.BlockSpec((YB, LZ, C, NX), lambda y: (y, 0, 0, 0))
    return pl.pallas_call(
        grad_kernel,
        grid=(LY // YB,),
        in_specs=[
            cell_spec,
            cell_spec,
            cell_spec,
            pl.BlockSpec((3, YB, LZ, NX), lambda y: (0, y, 0, 0)),
            whole((40, NX)),
            whole((C, 16)),
            whole((8, NX)),
        ],
        out_specs=[
            whole((GY, 2, 64, NX)),
            whole((64, NX)),
            whole((128, 128)),
        ],
        out_shape=[
            jax.ShapeDtypeStruct((GY, 2, 64, NX), BF16),
            jax.ShapeDtypeStruct((64, NX), BF16),
            jax.ShapeDtypeStruct((128, 128), F32),
        ],
        scratch_shapes=[
            pltpu.VMEM((4 * C, QZ * NX), BF16),
            pltpu.VMEM((2, 40 * 64, 128), F32),
            pltpu.VMEM((4 * C, 4 * C), F32),
            pltpu.VMEM((8, NX), F32),
            pltpu.VMEM((16, C), F32),
        ],
        compiler_params=params(),
        name="grad_dense",
    )(hidden, slope, cells, grad_b, forward, out_w, loss_rows)


DIRECTIONS = [(dy, dz) for dy in (-1, 0, 1) for dz in (-1, 0, 1) if dy or dz]


def halo_kernel(
    field, low, high, corner, y_low, y_high, z_low, z_high, corner_out, send, recv
):
    g, h = lax.axis_index("gy"), lax.axis_index("gz")

    def piece(dy, dz):
        if dz == 0:
            start = LY - 2 if dy > 0 else 0
            return field.at[:, pl.ds(start, 2)], (y_low if dy > 0 else y_high)
        if dy == 0:
            return (high, z_low) if dz > 0 else (low, z_high)
        index = (2 if dy > 0 else 0) + (1 if dz > 0 else 0)
        return corner.at[index], corner_out.at[3 - index]

    def exists(dy, dz):
        y, z = g + dy, h + dz
        return jnp.logical_and(
            jnp.logical_and(y >= 0, y < GY), jnp.logical_and(z >= 0, z < GZ)
        )

    def copy(index):
        dy, dz = DIRECTIONS[index]
        src, dst = piece(dy, dz)
        return pltpu.make_async_remote_copy(
            src_ref=src, dst_ref=dst, send_sem=send.at[index], recv_sem=recv.at[index],
            device_id={"gy": g + dy, "gz": h + dz}, device_id_type=MESH,
        )

    barrier = pltpu.get_barrier_semaphore()
    for dy, dz in DIRECTIONS:

        @pl.when(exists(dy, dz))
        def _(dy=dy, dz=dz):
            pl.semaphore_signal(
                barrier, inc=1, device_id={"gy": g + dy, "gz": h + dz}, device_id_type=MESH
            )

    y_sides = jnp.where(g > 0, 1, 0) + jnp.where(g < GY - 1, 1, 0)
    z_sides = jnp.where(h > 0, 1, 0) + jnp.where(h < GZ - 1, 1, 0)
    pl.semaphore_wait(barrier, (y_sides + 1) * (z_sides + 1) - 1)
    for index in range(8):

        @pl.when(exists(*DIRECTIONS[index]))
        def _(index=index):
            copy(index).start()

    for index in range(8):
        dy, dz = DIRECTIONS[index]

        @pl.when(exists(dy, dz))
        def _(index=index):
            copy(index).wait_send()

        @pl.when(exists(-dy, -dz))
        def _(index=index):
            copy(index).wait_recv()


def halo(collective_id, field, low, high, corner):
    side = jax.ShapeDtypeStruct((3, 2, LZ, NX), F32)
    edge = jax.ShapeDtypeStruct((3, 32, NX), F32)
    return pl.pallas_call(
        halo_kernel,
        out_shape=[side, side, edge, edge, jax.ShapeDtypeStruct((4, 8, NX), F32)],
        in_specs=[ANY] * 4,
        out_specs=[ANY] * 5,
        scratch_shapes=[pltpu.SemaphoreType.DMA((8,))] * 2,
        compiler_params=pltpu.CompilerParams(
            collective_id=collective_id, has_side_effects=True
        ),
        name="halo",
    )(field, low, high, corner)


def cell_loss(field_b, slope_x, slope_y, slope_z):
    current_x = slope_y[2] - slope_z[1]
    current_y = slope_z[0] - slope_x[2]
    current_z = slope_x[1] - slope_y[0]
    force_x = current_y * field_b[2] - current_z * field_b[1]
    force_y = current_z * field_b[0] - current_x * field_b[2]
    force_z = current_x * field_b[1] - current_y * field_b[0]
    spread = slope_x[0] + slope_y[1] + slope_z[2]
    strength = field_b[0] * field_b[0] + field_b[1] * field_b[1] + field_b[2] * field_b[2] + 1.0
    return (force_x * force_x + force_y * force_y + force_z * force_z) / strength + spread * spread


def stencil_kernel(
    place_ref, field_ref, y_low_ref, y_high_ref, z_low_ref, z_high_ref, corner_ref,
    grad_ref, loss_ref, wide, own, slopes,
):
    g, h = place_ref[0], place_ref[1]
    zero_rows = jnp.zeros((8, NX), F32)

    def kept(present, value):
        return jnp.where(present, value, jnp.zeros_like(value))

    for b in range(3):
        wide[b, 2:18, 8:24, :] = field_ref[b]
        wide[b, 0:2, 8:24, :] = kept(g > 0, y_low_ref[b])
        wide[b, 18:20, 8:24, :] = kept(g < GY - 1, y_high_ref[b])
        for plane in (0, 1, 18, 19):
            wide[b, plane, 0:8, :] = zero_rows
            wide[b, plane, 24:32, :] = zero_rows
        for y in range(LY):
            wide[b, y + 2, 0:8, :] = zero_rows
            wide[b, y + 2, 24:32, :] = zero_rows
            wide[b, y + 2, 6:8, :] = kept(h > 0, z_low_ref[b, 2 * y : 2 * y + 2, :])
            wide[b, y + 2, 24:26, :] = kept(h < GZ - 1, z_high_ref[b, 2 * y : 2 * y + 2, :])
        for index in range(4):
            y_side = g < GY - 1 if index // 2 else g > 0
            z_side = h < GZ - 1 if index % 2 else h > 0
            row = 24 if index % 2 else 7
            wide[b, 18 if index // 2 else 1, row : row + 1, :] = kept(
                jnp.logical_and(y_side, z_side), corner_ref[index, b : b + 1, :]
            )
    lane = lax.broadcasted_iota(jnp.int32, (32, NX), 1)
    row = lax.broadcasted_iota(jnp.int32, (32, NX), 0)
    z_cell = h * LZ + row - 8
    weight = jnp.where((z_cell >= 0) & (z_cell < NZ), 1.0 / CELLS, 0.0).astype(F32)
    inner = (row >= 8) & (row < 24)

    def x_diff(value):
        after = jnp.where(lane == NX - 1, 0.0, pltpu.roll(value, NX - 1, 1))
        before = jnp.where(lane == 0, 0.0, pltpu.roll(value, 1, 1))
        return (after - before) * 0.5

    def z_diff(value):
        return (pltpu.roll(value, 31, 0) - pltpu.roll(value, 1, 0)) * 0.5

    def one(plane, loss):
        cells = tuple(wide[b, plane] for b in range(3))
        slope_x = tuple(x_diff(value) for value in cells)
        slope_y = tuple((wide[b, plane + 1] - wide[b, plane - 1]) * 0.5 for b in range(3))
        slope_z = tuple(z_diff(value) for value in cells)
        terms, pullback = jax.vjp(cell_loss, cells, slope_x, slope_y, slope_z)
        y_cell = g * LY + plane - 2
        y_inside = jnp.logical_and(y_cell >= 0, y_cell < NY)
        grad_own, grad_x, grad_y, grad_z = pullback(jnp.where(y_inside, weight, 0.0))
        for b in range(3):
            own[b, plane - 1] = grad_own[b] - x_diff(grad_x[b]) - z_diff(grad_z[b])
            slopes[b, plane - 1] = grad_y[b]
        counted = jnp.logical_and(plane >= 2, plane < 18)
        return loss + jnp.where(jnp.logical_and(inner, counted), terms, 0.0)

    loss = lax.fori_loop(1, 19, one, jnp.zeros((32, NX), F32))
    total_loss = loss

    def finish(y, sums):
        result = []
        for b in range(3):
            grad = own[b, y + 1, 8:24, :] + (
                slopes[b, y, 8:24, :] - slopes[b, y + 2, 8:24, :]
            ) * 0.5
            grad_ref[b, y] = grad
            result.append(sums[b] + grad)
        return tuple(result)

    sums = lax.fori_loop(0, LY, finish, tuple(jnp.zeros((LZ, NX), F32) for _ in range(3)))
    loss_ref[...] = jnp.zeros_like(loss_ref)
    for index, value in enumerate((total_loss,) + sums):
        loss_ref[index : index + 1, :] = jnp.sum(value, axis=0, keepdims=True)


def stencil(place, field, *halos):
    vmem = pl.BlockSpec(memory_space=pltpu.VMEM)
    return pl.pallas_call(
        stencil_kernel,
        in_specs=[pl.BlockSpec(memory_space=pltpu.SMEM)] + [vmem] * 6,
        out_specs=[vmem] * 2,
        out_shape=[
            jax.ShapeDtypeStruct((3, LY, LZ, NX), F32),
            jax.ShapeDtypeStruct((8, NX), F32),
        ],
        scratch_shapes=[
            pltpu.VMEM((3, 20, 32, NX), F32),
            pltpu.VMEM((3, 18, 32, NX), F32),
            pltpu.VMEM((3, 18, 32, NX), F32),
        ],
        compiler_params=params(),
        name="stencil",
    )(place, field, *halos)


def on_device(field_in, spectral_weight, point_weight, point_bias, out_weight, out_bias):
    place = jnp.stack([lax.axis_index("gy"), lax.axis_index("gz")]).astype(jnp.int32)
    cells, rows, odd = x_transform(field_in)
    rows, odd = swap("gy", GY, 1, (FAR, NEAR), ("swap", rows), ("to0", odd))
    modes_in = to_kx(to_modes(2, SCALE, rows, odd).astype(BF16))

    mixed = jnp.einsum(
        "abkpi,abkio->abkpo", modes_in, spectral_weight, preferred_element_type=F32
    )
    real = mixed[..., 0, :C] - mixed[..., 1, C:]
    imag = mixed[..., 0, C:] + mixed[..., 1, :C]
    modes_out = jnp.stack([real, imag], axis=3)

    rows, odd = from_modes(4, from_kx(modes_out))
    rows, odd = swap("gy", GY, 6, (NEAR, FAR), ("swap", rows), ("from0", odd))

    hidden, slope, field_b, *edges = dense(
        rows, odd, cells, point_weight, point_bias, out_weight, out_bias
    )
    grad_b, loss_rows = stencil(place, field_b, *halo(10, field_b, *edges))
    rows, odd, small = grad_dense(hidden, slope, cells, grad_b, out_weight, loss_rows)
    small = small.reshape(GY, 8, 128)
    rows, odd, small = swap("gy", GY, 7, (FAR, NEAR), ("swap", rows), ("to0", odd), ("swap", small))
    dealt, small = to_modes(8, 1.0, rows, odd, small)
    small = small.reshape(128, 128)
    grad_modes = to_kx(dealt.astype(BF16))
    grad_spectral = weight_grad(modes_in, grad_modes).reshape(4, 2, M, C, 2 * C)
    scalars = jnp.sum(small[80:84], axis=1)
    return (
        scalars[0] / CELLS,
        grad_spectral,
        small[:C, :C],
        small[64, :C],
        small[72:75, :C].T,
        scalars[1:4],
    )


def solution(mesh):
    return jax.shard_map(
        on_device,
        mesh=mesh,
        in_specs=(P(None, "gy", "gz", None), P("gz", "gy", None, None, None), P(), P(), P(), P()),
        out_specs=(P(), P("gz", "gy", None, None, None), P(), P(), P(), P()),
        check_vma=False,
    )
```

```python
import functools
import math

import jax
import jax.numpy as jnp
import numpy as np
from jax import lax
from jax.experimental import pallas as pl
from jax.experimental.pallas import tpu as pltpu
from jax.sharding import PartitionSpec as P

NX, NY, NZ = 256, 256, 128
M = 32
C = 64
GY, GZ = 16, 8
LY, LZ = 16, 16
YB = 2
QZ = 4
F32, BF16 = jnp.float32, jnp.bfloat16
SCALE = math.sqrt(M * M * M / (NX * NY * NZ))
CELLS = NX * NY * NZ
DENSITY = 1.0 / math.sqrt(math.pi)
MESH = pl.DeviceIdType.MESH
ANY = pl.BlockSpec(memory_space=pl.ANY)
NEAR = pl.BlockSpec(memory_space=pltpu.VMEM)
FAR = pl.BlockSpec(memory_space=pltpu.HBM)


def np_table(length):
    mode = np.arange(M)
    wave = np.where(mode < M // 2, mode, mode - M)
    product = (np.arange(length)[:, None] * wave[None, :]) % length
    phases = product.astype(np.float64) * (2.0 * math.pi / length)
    return np.cos(phases), np.sin(phases)


@functools.lru_cache(None)
def tables():
    cos_x, sin_x = np_table(NX)
    forward = np.zeros((40, NX))
    forward[:16] = cos_x[:, :16].T
    forward[16] = cos_x[:, 16]
    forward[17:32] = sin_x[:, 1:16].T
    forward[32] = sin_x[:, 16]
    inverse = np.zeros((40, NX))
    inverse[33:36] = 1.0
    inverse[0:32:2] = forward[:16]
    inverse[1:32:2] = forward[16:32]
    inverse[32] = forward[32]
    cos_y, sin_y = np_table(NY)
    y_rows = np.kron(np.concatenate([cos_y, sin_y], axis=1).T, np.eye(QZ))
    cos_z, sin_z = np_table(NZ)
    z_rows = []
    for table in (cos_z, sin_z):
        cells = table.reshape(GZ, QZ, 4, M)
        for inner in range(4):
            part = cells[:, :, inner, :].reshape(GZ, QZ, GZ, 4)
            full = np.zeros((GZ, 2, 4, 2, GZ, 4, QZ))
            for gs in range(2):
                for ky2 in range(2):
                    full[:, gs, :, ky2, :, gs * 2 + ky2, :] = part.transpose(2, 3, 0, 1)
            z_rows.append(full.reshape(128, 128))
    z_rows = np.stack(z_rows).reshape(2, 4, 128, 128)
    return forward, inverse, y_rows, z_rows


def const(value):
    return jnp.asarray(value, BF16)


NT = (((1,), (1,)), ((), ()))
TN = (((0,), (0,)), ((), ()))


def dot(left, right, dims=(((1,), (0,)), ((), ()))):
    return lax.dot_general(left, right, dims, preferred_element_type=F32)


def whole(shape):
    return pl.BlockSpec(shape, lambda *_: (0,) * len(shape))


def params(limit=50 << 20):
    return pltpu.CompilerParams(vmem_limit_bytes=limit)


def swap_kernel(axis, count, modes, *refs):
    size = len(modes)
    srcs, dsts, sends, recvs = [refs[i * size : i * size + size] for i in range(4)]
    local = refs[4 * size]
    me = lax.axis_index(axis)
    barrier = pltpu.get_barrier_semaphore()
    for step in range(1, count):
        pl.semaphore_signal(
            barrier, inc=1, device_id={axis: (me + step) % count}, device_id_type=MESH
        )
    pl.semaphore_wait(barrier, count - 1)

    def remote(src, dst, send, recv, peer):
        return pltpu.make_async_remote_copy(
            src_ref=src, dst_ref=dst, send_sem=send, recv_sem=recv,
            device_id={axis: peer}, device_id_type=MESH,
        )

    copies, early, late = [], [], []
    for index, mode in enumerate(modes):
        src, dst, send, recv = srcs[index], dsts[index], sends[index], recvs[index]
        if mode == "to0":

            def begin(step, src=src, dst=dst, send=send, recv=recv):
                @pl.when(jnp.logical_and(me != 0, me == step))
                def _():
                    remote(src, dst.at[me], send.at[0], recv.at[me], 0).start()

            early.append(begin)

            @pl.when(me == 0)
            def _(src=src, dst=dst, index=index):
                pltpu.make_async_copy(src, dst.at[0], local.at[index]).start()

            def finish(src=src, dst=dst, send=send, recv=recv, index=index):
                @pl.when(me != 0)
                def _():
                    remote(src, dst.at[me], send.at[0], recv.at[me], 0).wait_send()

                @pl.when(me == 0)
                def _():
                    pltpu.make_async_copy(src, dst.at[0], local.at[index]).wait()
                    for k in range(1, count):
                        remote(src, dst.at[k], send.at[0], recv.at[k], k).wait_recv()

            late.append(finish)
        elif mode == "from0":

            @pl.when(me == 0)
            def _(src=src, dst=dst, send=send, recv=recv, index=index):
                pltpu.make_async_copy(src.at[0], dst, local.at[index]).start()
                for k in range(1, count):
                    remote(src.at[k], dst, send.at[k], recv.at[0], k).start()

            def finish(src=src, dst=dst, send=send, recv=recv, index=index):
                @pl.when(me == 0)
                def _():
                    pltpu.make_async_copy(src.at[0], dst, local.at[index]).wait()
                    for k in range(1, count):
                        remote(src.at[k], dst, send.at[k], recv.at[0], k).wait_send()

                @pl.when(me != 0)
                def _():
                    remote(src.at[0], dst, send.at[0], recv.at[0], 0).wait_recv()

            late.append(finish)
        else:
            piece = (lambda p, src=src: src.at[p]) if mode == "swap" else (lambda p, src=src: src)
            copies.append((0, pltpu.make_async_copy(piece(me), dst.at[me], local.at[index])))
            for step in range(1, count):
                peer = (me + step) % count
                copies.append(
                    (step, remote(piece(peer), dst.at[me], send.at[step], recv.at[step], peer))
                )
    for step in range(count):
        for at, copy in copies:
            if at == step:
                copy.start()
        for begin in early:
            begin(step)
    copies = [copy for _, copy in copies]
    for copy in copies:
        copy.wait()
    for finish in late:
        finish()


def swap(axis, count, collective_id, spaces, *operands):
    modes = tuple(mode for mode, _ in operands)
    args = [value for _, value in operands]
    outs = []
    for mode, value in operands:
        shape = value.shape
        if mode in ("all", "to0"):
            shape = (count,) + shape
        elif mode == "from0":
            shape = shape[1:]
        outs.append(jax.ShapeDtypeStruct(shape, value.dtype))
    size = len(args)
    result = pl.pallas_call(
        functools.partial(swap_kernel, axis, count, modes),
        out_shape=outs,
        in_specs=[spaces[0]] * size,
        out_specs=[spaces[1]] * size,
        scratch_shapes=[pltpu.SemaphoreType.DMA((count,))] * (2 * size)
        + [pltpu.SemaphoreType.DMA((size,))],
        compiler_params=pltpu.CompilerParams(
            collective_id=collective_id, has_side_effects=True, vmem_limit_bytes=16 << 20
        ),
        name=f"swap_{collective_id}",
    )(*args)
    return result if size > 1 else result[0]


def emit_rows(rows_ref, out_ref, extra_ref):
    for half in range(2):
        lanes = slice(half * 128, half * 128 + 128)
        for g in range(GY):
            for part in range(2):
                start = (part * GY + g) * 64
                out_ref[g, part, :, lanes] = rows_ref[half, start : start + 64, :].astype(BF16)
        extra_ref[:, lanes] = rows_ref[half, 2048:2112, :].astype(BF16)


def put_rows(rows_ref, start, value):
    for half in range(2):
        rows_ref[half, pl.ds(start, 40, stride=64), :] = value[:, half * 128 : half * 128 + 128]


def x_kernel(field_ref, table_ref, cells_ref, out_ref, extra_ref, stage, rows):
    step = pl.program_id(0)

    def plane(k, carry):
        for half in range(2):
            lanes = slice(half * 128, half * 128 + 128)
            stage[half] = field_ref[:, k, :, lanes].astype(F32).reshape(C * LZ, 128)
            for z in range(LZ):
                cells_ref[k, z, :, lanes] = stage[half, pl.ds(z, C, stride=LZ), :].astype(BF16)
        for q in range(QZ):
            block = cells_ref[k, q * 4 : q * 4 + 4].reshape(4 * C, NX)
            put_rows(rows, (step * YB + k) * QZ + q, dot(table_ref[...], block, NT))
        return carry

    lax.fori_loop(0, YB, plane, 0)

    @pl.when(step == LY // YB - 1)
    def _():
        emit_rows(rows, out_ref, extra_ref)


def x_transform(field_in):
    forward = const(tables()[0])
    return pl.pallas_call(
        x_kernel,
        grid=(LY // YB,),
        in_specs=[
            pl.BlockSpec((C, YB, LZ, NX), lambda y: (0, y, 0, 0)),
            whole((40, NX)),
        ],
        out_specs=[
            pl.BlockSpec((YB, LZ, C, NX), lambda y: (y, 0, 0, 0)),
            whole((GY, 2, 64, NX)),
            whole((64, NX)),
        ],
        out_shape=[
            jax.ShapeDtypeStruct((LY, LZ, C, NX), BF16),
            jax.ShapeDtypeStruct((GY, 2, 64, NX), BF16),
            jax.ShapeDtypeStruct((64, NX), BF16),
        ],
        scratch_shapes=[pltpu.VMEM((2, C * LZ, 128), F32), pltpu.VMEM((2, 40 * 64, 128), F32)],
        compiler_params=params(),
        name="x_transform",
    )(field_in, forward)


def y_body(first, src_ref, extra_ref, table_ref, out_ref):
    sums = []
    for part in range(2):
        sums.append(dot(table_ref[...], src_ref[:, part].reshape(GY * 64, NX)))
    sums.append(dot(table_ref[...], extra_ref[...].reshape(GY * 64, NX)))
    zero = jnp.zeros((128, NX), F32)
    cc, cs = sums[0][:128], sums[0][128:]
    sc, ss = sums[1][:128], sums[1][128:]
    ec, es = sums[2][:128], sums[2][128:]
    pc, ps = jnp.where(first, zero, sc), jnp.where(first, zero, ss)
    nc, ns = jnp.where(first, sc, cc), jnp.where(first, ss, cs)
    mc, ms = jnp.where(first, ec, -sc), jnp.where(first, es, -ss)
    parts = (cc - ps, -(cs + pc), nc - ms, -(ns + mc))
    for index, part in enumerate(parts):
        out_ref[:, index] = part.astype(BF16).reshape(GZ, 16, NX)


def y_back_body(first, src_ref, table_ref, out_ref, extra_ref):
    ar, ai, br, bi = [
        src_ref[:, part].reshape(128, NX).astype(F32) for part in range(4)
    ]
    rows = (
        (jnp.where(first, ar, ar + br), jnp.where(first, -ai, -(ai + bi))),
        (jnp.where(first, br, bi - ai), jnp.where(first, -bi, br - ar)),
        (jnp.where(first, -bi, 0.0), jnp.where(first, -br, 0.0)),
    )
    for part, (upper, lower) in enumerate(rows):
        operand = jnp.concatenate([upper, lower], axis=0).astype(BF16)
        result = dot(table_ref[...], operand).astype(BF16).reshape(GY, 64, NX)
        if part < 2:
            out_ref[:, part] = result
        else:
            extra_ref[...] = result


def z_body(factor, src_ref, table_ref, out_ref):
    for m in range(2):
        sums = []
        for p in range(2):
            block = src_ref[:, m * 2 + p].reshape(128, NX)
            pair = []
            for t in range(2):
                total = None
                for inner in range(4):
                    term = dot(table_ref[t, inner], block[:, inner * C : inner * C + C])
                    total = term if total is None else total + term
                pair.append(total)
            sums.append(pair)
        real = sums[0][0] + sums[1][1]
        imag = sums[1][0] - sums[0][1]
        out_ref[:, :, m * 128 : m * 128 + 128] = (
            jnp.concatenate([real, imag], axis=1) * factor
        ).reshape(GY, 8, 128)


def z_back_body(src_ref, table_ref, out_ref):
    for m in range(2):
        block = src_ref[:, :, m * 128 : m * 128 + 128].reshape(128, 128).astype(BF16)
        real, imag = [], []
        for inner in range(4):
            cos_part = dot(table_ref[0, inner], block)
            sin_part = dot(table_ref[1, inner], block)
            real.append(cos_part[:, :C] - sin_part[:, C:])
            imag.append(cos_part[:, C:] + sin_part[:, :C])
        for p, pieces in enumerate((real, imag)):
            full = jnp.concatenate(pieces, axis=1).astype(BF16)
            out_ref[:, m * 2 + p] = full.reshape(GZ, 16, NX)


def mode_places():
    g, h = lax.axis_index("gy"), lax.axis_index("gz")
    owners = [(2 * h + j % 2, j // 2) for j in range(GY)]
    holders = [(k, g // 2) for k in range(GY)]
    return g, h, owners, holders


def greet(g, h, sources, with_gy):
    barrier = pltpu.get_barrier_semaphore()
    for step in range(1, GZ):
        pl.semaphore_signal(
            barrier, inc=1, device_id={"gz": (h + step) % GZ}, device_id_type=MESH
        )
    if with_gy:
        for step in range(1, GY):
            pl.semaphore_signal(
                barrier, inc=1, device_id={"gy": (g + step) % GY}, device_id_type=MESH
            )
    for y, z in sources:

        @pl.when(jnp.logical_not(jnp.logical_and(y == g, z == h)))
        def _(y=y, z=z):
            pl.semaphore_signal(barrier, inc=1, device_id={"gy": y, "gz": z}, device_id_type=MESH)


def await_greetings(g, h, with_gy):
    fixed = GZ - 1 + (GY - 1 if with_gy else 0)
    pl.semaphore_wait(
        pltpu.get_barrier_semaphore(), jnp.where(g // 2 == h, GY - 1, GY) + fixed
    )


def spread(axis, count, me, piece, dst, send, recv, local):
    copies = [pltpu.make_async_copy(piece(me), dst.at[me], local)]
    for step in range(1, count):
        peer = (me + step) % count
        copies.append(
            pltpu.make_async_remote_copy(
                src_ref=piece(peer), dst_ref=dst.at[me],
                send_sem=send.at[step], recv_sem=recv.at[step],
                device_id={axis: peer}, device_id_type=MESH,
            )
        )
    for copy in copies:
        copy.start()
    return copies


def deal(g, h, targets, sources, slot, src, dst, send, recv, local):
    def is_me(device):
        return jnp.logical_and(device[0] == g, device[1] == h)

    def remote(j, device, landing, arrived):
        return pltpu.make_async_remote_copy(
            src_ref=src.at[j], dst_ref=dst.at[landing],
            send_sem=send.at[j], recv_sem=recv.at[arrived],
            device_id={"gy": device[0], "gz": device[1]}, device_id_type=MESH,
        )

    for j in range(GY):
        mine = is_me(targets[j])

        @pl.when(jnp.logical_not(mine))
        def _(j=j):
            remote(j, targets[j], slot, slot).start()

        @pl.when(mine)
        def _(j=j):
            copy = pltpu.make_async_copy(src.at[j], dst.at[slot], local)
            copy.start()
            copy.wait()

    for j in range(GY):

        @pl.when(jnp.logical_not(is_me(targets[j])))
        def _(j=j):
            remote(j, targets[j], slot, slot).wait_send()

        @pl.when(jnp.logical_not(is_me(sources[j])))
        def _(j=j):
            remote(j, sources[j], j, j).wait_recv()


def to_modes_kernel(factor, with_small, *refs):
    if with_small:
        (rows, extra, y_table, z_table, small, dealt, small_out, y_out, z_in, z_out,
         send, recv, send2, recv2, local, small_a, small_b, small_c,
         send3, recv3, send4, recv4) = refs
    else:
        (rows, extra, y_table, z_table, dealt, y_out, z_in, z_out,
         send, recv, send2, recv2, local) = refs
    g, h, owners, holders = mode_places()
    greet(g, h, holders, with_small)
    y_body(g == 0, rows, extra, y_table, y_out)
    if with_small:
        small_a[...] = jnp.sum(small[...], axis=0)
    await_greetings(g, h, with_small)
    copies = spread("gz", GZ, h, lambda p: y_out.at[p], z_in, send, recv, local.at[0])
    if with_small:
        copies += spread("gz", GZ, h, lambda p: small_a, small_b, send3, recv3, local.at[1])
    for copy in copies:
        copy.wait()
    z_body(factor, z_in, z_table, z_out)
    copies = []
    if with_small:
        small_c[...] = jnp.sum(small_b[...], axis=0)
        copies = spread("gy", GY, g, lambda p: small_c, small_out, send4, recv4, local.at[2])
    deal(g, h, owners, holders, g, z_out, dealt, send2, recv2, local.at[3])
    for copy in copies:
        copy.wait()


def to_modes(collective_id, factor, rows, extra, small=None):
    vmem = pl.BlockSpec(memory_space=pltpu.VMEM)
    args = [rows, extra, const(tables()[2]), const(tables()[3])]
    outs = [jax.ShapeDtypeStruct((GY, 8, 256), F32)]
    block = pltpu.VMEM((GZ, 4, 16, NX), BF16)
    gz_sems = [pltpu.SemaphoreType.DMA((GZ,))] * 2
    gy_sems = [pltpu.SemaphoreType.DMA((GY,))] * 2
    scratch = [block, block, pltpu.VMEM((GY, 8, 256), F32)]
    scratch += gz_sems + gy_sems + [pltpu.SemaphoreType.DMA((4,))]
    if small is not None:
        args.append(small)
        outs.append(jax.ShapeDtypeStruct((GY, 8, 128), F32))
        scratch += [
            pltpu.VMEM((8, 128), F32),
            pltpu.VMEM((GZ, 8, 128), F32),
            pltpu.VMEM((8, 128), F32),
        ]
        scratch += gz_sems + gy_sems
    result = pl.pallas_call(
        functools.partial(to_modes_kernel, factor, small is not None),
        out_shape=outs,
        in_specs=[vmem] * len(args),
        out_specs=[ANY] * len(outs),
        scratch_shapes=scratch,
        compiler_params=pltpu.CompilerParams(
            collective_id=collective_id, has_side_effects=True, vmem_limit_bytes=40 << 20
        ),
        name=f"to_modes_{collective_id}",
    )(*args)
    return result if small is not None else result[0]


def from_modes_kernel(
    modes, y_table, z_table, rows, extra, landed, z_out, y_in, send, recv, send2, recv2, local
):
    g, h, owners, holders = mode_places()
    greet(g, h, owners, False)
    await_greetings(g, h, False)
    deal(g, h, holders, owners, h * 2 + g % 2, modes, landed, send2, recv2, local.at[1])
    z_back_body(landed, z_table, z_out)
    copies = spread("gz", GZ, h, lambda p: z_out.at[p], y_in, send, recv, local.at[0])
    for copy in copies:
        copy.wait()
    y_back_body(g == 0, y_in, y_table, rows, extra)


def from_modes(collective_id, modes):
    vmem = pl.BlockSpec(memory_space=pltpu.VMEM)
    block = pltpu.VMEM((GZ, 4, 16, NX), BF16)
    return pl.pallas_call(
        from_modes_kernel,
        out_shape=[
            jax.ShapeDtypeStruct((GY, 2, 64, NX), BF16),
            jax.ShapeDtypeStruct((GY, 64, NX), BF16),
        ],
        in_specs=[vmem] * 3,
        out_specs=[vmem] * 2,
        scratch_shapes=[pltpu.VMEM((GY, 8, 256), F32), block, block]
        + [pltpu.SemaphoreType.DMA((GZ,))] * 2
        + [pltpu.SemaphoreType.DMA((GY,))] * 2
        + [pltpu.SemaphoreType.DMA((2,))],
        compiler_params=pltpu.CompilerParams(
            collective_id=collective_id, has_side_effects=True, vmem_limit_bytes=40 << 20
        ),
        name=f"from_modes_{collective_id}",
    )(modes, const(tables()[2].T), const(tables()[3].transpose(0, 1, 3, 2)))


def to_kx(dealt):
    split = dealt.reshape(GY, 4, 2, 2, 2, C)
    plus, minus = split[:, :, :, 0], split[:, :, :, 1]
    order = jnp.concatenate([plus, minus[:1], minus[1:][::-1]], axis=0)
    return order.transpose(1, 2, 0, 3, 4)


def from_kx(modes):
    order = modes.transpose(2, 0, 1, 3, 4)
    minus = jnp.concatenate([order[16:17], order[17:][::-1]], axis=0)
    return jnp.stack([order[:16], minus], axis=3).reshape(GY, 8, 256)


def weight_grad_kernel(u_ref, g_ref, mask_ref, out_ref):
    for block in range(4):
        right = jnp.concatenate([g_ref[block]] * 8, axis=1) * mask_ref[...]
        result = dot(u_ref[block], right, TN)
        for mode in range(8):
            out_ref[0, block * 8 + mode] = result[:, mode * 128 : mode * 128 + 128]


def weight_grad(modes_in, grad_modes):
    u = modes_in.reshape(M, 16, C)
    real, imag = grad_modes[..., 0, :], grad_modes[..., 1, :]
    g = jnp.stack(
        [jnp.concatenate([real, imag], axis=-1), jnp.concatenate([imag, -real], axis=-1)], axis=3
    ).reshape(M, 16, 128)
    mask = const(np.kron(np.eye(8), np.ones((2, 128))))
    return pl.pallas_call(
        weight_grad_kernel,
        grid=(8,),
        in_specs=[
            pl.BlockSpec((4, 16, C), lambda i: (i, 0, 0)),
            pl.BlockSpec((4, 16, 128), lambda i: (i, 0, 0)),
            whole((16, 1024)),
        ],
        out_specs=pl.BlockSpec((1, M, C, 128), lambda i: (i, 0, 0, 0)),
        out_shape=jax.ShapeDtypeStruct((8, M, C, 128), F32),
        compiler_params=params(),
        name="weight_grad",
    )(u, g, mask)


def dense_kernel(
    rows_ref, odd_ref, cells_ref, table_ref, point_ref, bias_ref, out_w_ref, out_b_ref,
    hidden_ref, slope_ref, field_ref, low_ref, high_ref, corner_ref, rows,
):
    step = pl.program_id(0)

    @pl.when(step == 0)
    def _():
        corner_ref[...] = jnp.zeros_like(corner_ref)
        for half in range(2):
            lanes = slice(half * 128, half * 128 + 128)
            for g in range(GY * 2):
                rows[half, g * 64 : g * 64 + 64, :] = rows_ref[g, :, lanes].astype(F32)
            rows[half, 2048:2112, :] = odd_ref[:, lanes].astype(F32)
            rest = bias_ref[...]
            for part in range(3):
                piece = rest.astype(BF16).astype(F32)
                start = 2112 + part * 64
                rows[half, start : start + 64, :] = jnp.broadcast_to(piece, (64, 128))
                rest = rest - piece
            rows[half, 2304:2560, :] = jnp.zeros((256, 128), F32)

    def plane(k, carry):
        y = step * YB + k
        for q in range(QZ):
            picked = jnp.concatenate(
                [rows[half, pl.ds(y * QZ + q, 40, stride=64), :] for half in range(2)], axis=1
            ).astype(BF16)
            spectral = dot(picked, table_ref[...], TN)
            for inner in range(4):
                z = q * 4 + inner
                pre = spectral[inner * C : inner * C + C] + dot(point_ref[...], cells_ref[k, z])
                scaled = pre * math.sqrt(0.5)
                normal_cdf = 0.5 * lax.erf(scaled) + 0.5
                decay = jnp.exp2(scaled * scaled * -math.log2(math.e))
                hidden = (pre * normal_cdf).astype(BF16)
                hidden_ref[k, z] = hidden
                slope_ref[k, z] = (normal_cdf + scaled * DENSITY * decay).astype(BF16)
                b_rows = dot(out_w_ref[...], hidden)
                for b in range(3):
                    field_ref[b, k, z : z + 1, :] = b_rows[b : b + 1] + out_b_ref[b]
        for b in range(3):
            for i in range(2):
                z = LZ - 2 + i
                low_ref[b, pl.ds(y * 2 + i, 1), :] = field_ref[b, k, i : i + 1, :]
                high_ref[b, pl.ds(y * 2 + i, 1), :] = field_ref[b, k, z : z + 1, :]
        return carry

    lax.fori_loop(0, YB, plane, 0)
    for y_edge in range(2):

        @pl.when(step == y_edge * (LY // YB - 1))
        def _(y_edge=y_edge):
            for b in range(3):
                for z_edge in range(2):
                    z = z_edge * (LZ - 1)
                    corner_ref[y_edge * 2 + z_edge, b : b + 1, :] = field_ref[
                        b, y_edge * (YB - 1), z : z + 1, :
                    ]


def dense(rows, odd, cells, point_weight, point_bias, out_weight, out_bias):
    out_w = jnp.pad(out_weight.T, ((0, 5), (0, 0)))
    cell_spec = pl.BlockSpec((YB, LZ, C, NX), lambda y: (y, 0, 0, 0))
    cell_shape = jax.ShapeDtypeStruct((LY, LZ, C, NX), BF16)
    return pl.pallas_call(
        dense_kernel,
        grid=(LY // YB,),
        in_specs=[
            whole((GY * 2, 64, NX)),
            whole((64, NX)),
            cell_spec,
            whole((40, NX)),
            whole((C, C)),
            whole((1, 128)),
            whole((8, C)),
            pl.BlockSpec(memory_space=pltpu.SMEM),
        ],
        out_specs=[
            cell_spec,
            cell_spec,
            pl.BlockSpec((3, YB, LZ, NX), lambda y: (0, y, 0, 0)),
            whole((3, 32, NX)),
            whole((3, 32, NX)),
            whole((4, 8, NX)),
        ],
        out_shape=[
            cell_shape,
            cell_shape,
            jax.ShapeDtypeStruct((3, LY, LZ, NX), F32),
            jax.ShapeDtypeStruct((3, 32, NX), F32),
            jax.ShapeDtypeStruct((3, 32, NX), F32),
            jax.ShapeDtypeStruct((4, 8, NX), F32),
        ],
        scratch_shapes=[pltpu.VMEM((2, 40 * 64, 128), F32)],
        compiler_params=params(),
        name="dense",
    )(
        rows.reshape(GY * 2, 64, NX),
        odd,
        cells,
        const(tables()[1]),
        point_weight.T,
        jnp.concatenate([point_bias, point_bias])[None],
        out_w,
        out_bias,
    )


def grad_kernel(
    hidden_ref, slope_ref, cells_ref, grad_ref, table_ref, out_w_ref, loss_ref,
    rows_ref, odd_ref, small_ref,
    stage, rows, point_sum, bias_sum, out_sum,
):
    step = pl.program_id(0)

    @pl.when(step == 0)
    def _():
        point_sum[...] = jnp.zeros_like(point_sum)
        bias_sum[...] = jnp.zeros_like(bias_sum)
        out_sum[...] = jnp.zeros_like(out_sum)

    def plane(k, carry):
        out_total, bias_total = None, None
        for q in range(QZ):
            for inner in range(4):
                z = q * 4 + inner
                grad = jnp.concatenate(
                    [grad_ref[b, k, z : z + 1, :] for b in range(3)] + [jnp.zeros((5, NX), F32)],
                    axis=0,
                )
                upper = grad.astype(BF16)
                lower = (grad - upper.astype(F32)).astype(BF16)
                both = jnp.concatenate([upper, lower], axis=0)
                grad_hidden = dot(out_w_ref[...], both)
                stage[inner * C : inner * C + C, q * NX : q * NX + NX] = (
                    grad_hidden * slope_ref[k, z].astype(F32)
                ).astype(BF16)
                out_term = dot(both, hidden_ref[k, z], NT)
                out_total = out_term if out_total is None else out_total + out_term
            x_rows = dot(table_ref[...], stage[:, q * NX : q * NX + NX], NT)
            put_rows(rows, (step * YB + k) * QZ + q, x_rows)
            bias_total = x_rows[0:8] if bias_total is None else bias_total + x_rows[0:8]
        out_sum[...] += out_total
        bias_sum[...] += bias_total
        cells = jnp.concatenate(
            [cells_ref[k, q * 4 : q * 4 + 4].reshape(4 * C, NX) for q in range(QZ)], axis=1
        )
        point_sum[...] += dot(cells, stage[...], NT)
        return carry

    lax.fori_loop(0, YB, plane, 0)

    @pl.when(step == LY // YB - 1)
    def _():
        emit_rows(rows, rows_ref, odd_ref)
        total = point_sum[0:C, 0:C]
        bias = bias_sum[0:1, 0:C]
        for inner in range(1, 4):
            span = slice(inner * C, inner * C + C)
            total = total + point_sum[span, span]
            bias = bias + bias_sum[0:1, span]
        small_ref[...] = jnp.zeros_like(small_ref)
        small_ref[0:C, 0:C] = total
        small_ref[64:65, 0:C] = bias
        small_ref[72:80, 0:C] = out_sum[0:8] + out_sum[8:16]
        small_ref[80:88, :] = loss_ref[:, 0:128] + loss_ref[:, 128:256]


def grad_dense(hidden, slope, cells, grad_b, out_weight, loss_rows):
    forward = const(tables()[0])
    out_w = jnp.pad(out_weight, ((0, 0), (0, 5)))
    out_w = jnp.concatenate([out_w, out_w], axis=1)
    cell_spec = pl.BlockSpec((YB, LZ, C, NX), lambda y: (y, 0, 0, 0))
    return pl.pallas_call(
        grad_kernel,
        grid=(LY // YB,),
        in_specs=[
            cell_spec,
            cell_spec,
            cell_spec,
            pl.BlockSpec((3, YB, LZ, NX), lambda y: (0, y, 0, 0)),
            whole((40, NX)),
            whole((C, 16)),
            whole((8, NX)),
        ],
        out_specs=[
            whole((GY, 2, 64, NX)),
            whole((64, NX)),
            whole((128, 128)),
        ],
        out_shape=[
            jax.ShapeDtypeStruct((GY, 2, 64, NX), BF16),
            jax.ShapeDtypeStruct((64, NX), BF16),
            jax.ShapeDtypeStruct((128, 128), F32),
        ],
        scratch_shapes=[
            pltpu.VMEM((4 * C, QZ * NX), BF16),
            pltpu.VMEM((2, 40 * 64, 128), F32),
            pltpu.VMEM((4 * C, 4 * C), F32),
            pltpu.VMEM((8, NX), F32),
            pltpu.VMEM((16, C), F32),
        ],
        compiler_params=params(),
        name="grad_dense",
    )(hidden, slope, cells, grad_b, forward, out_w, loss_rows)


DIRECTIONS = [(dy, dz) for dy in (-1, 0, 1) for dz in (-1, 0, 1) if dy or dz]


def halo_kernel(
    field, low, high, corner, y_low, y_high, z_low, z_high, corner_out, send, recv
):
    g, h = lax.axis_index("gy"), lax.axis_index("gz")

    def piece(dy, dz):
        if dz == 0:
            start = LY - 2 if dy > 0 else 0
            return field.at[:, pl.ds(start, 2)], (y_low if dy > 0 else y_high)
        if dy == 0:
            return (high, z_low) if dz > 0 else (low, z_high)
        index = (2 if dy > 0 else 0) + (1 if dz > 0 else 0)
        return corner.at[index], corner_out.at[3 - index]

    def exists(dy, dz):
        y, z = g + dy, h + dz
        return jnp.logical_and(
            jnp.logical_and(y >= 0, y < GY), jnp.logical_and(z >= 0, z < GZ)
        )

    def copy(index):
        dy, dz = DIRECTIONS[index]
        src, dst = piece(dy, dz)
        return pltpu.make_async_remote_copy(
            src_ref=src, dst_ref=dst, send_sem=send.at[index], recv_sem=recv.at[index],
            device_id={"gy": g + dy, "gz": h + dz}, device_id_type=MESH,
        )

    barrier = pltpu.get_barrier_semaphore()
    for dy, dz in DIRECTIONS:

        @pl.when(exists(dy, dz))
        def _(dy=dy, dz=dz):
            pl.semaphore_signal(
                barrier, inc=1, device_id={"gy": g + dy, "gz": h + dz}, device_id_type=MESH
            )

    y_sides = jnp.where(g > 0, 1, 0) + jnp.where(g < GY - 1, 1, 0)
    z_sides = jnp.where(h > 0, 1, 0) + jnp.where(h < GZ - 1, 1, 0)
    pl.semaphore_wait(barrier, (y_sides + 1) * (z_sides + 1) - 1)
    for index in range(8):

        @pl.when(exists(*DIRECTIONS[index]))
        def _(index=index):
            copy(index).start()

    for index in range(8):
        dy, dz = DIRECTIONS[index]

        @pl.when(exists(dy, dz))
        def _(index=index):
            copy(index).wait_send()

        @pl.when(exists(-dy, -dz))
        def _(index=index):
            copy(index).wait_recv()


def halo(collective_id, field, low, high, corner):
    side = jax.ShapeDtypeStruct((3, 2, LZ, NX), F32)
    edge = jax.ShapeDtypeStruct((3, 32, NX), F32)
    return pl.pallas_call(
        halo_kernel,
        out_shape=[side, side, edge, edge, jax.ShapeDtypeStruct((4, 8, NX), F32)],
        in_specs=[ANY] * 4,
        out_specs=[ANY] * 5,
        scratch_shapes=[pltpu.SemaphoreType.DMA((8,))] * 2,
        compiler_params=pltpu.CompilerParams(
            collective_id=collective_id, has_side_effects=True
        ),
        name="halo",
    )(field, low, high, corner)


def cell_loss(field_b, slope_x, slope_y, slope_z):
    current_x = slope_y[2] - slope_z[1]
    current_y = slope_z[0] - slope_x[2]
    current_z = slope_x[1] - slope_y[0]
    force_x = current_y * field_b[2] - current_z * field_b[1]
    force_y = current_z * field_b[0] - current_x * field_b[2]
    force_z = current_x * field_b[1] - current_y * field_b[0]
    spread = slope_x[0] + slope_y[1] + slope_z[2]
    strength = field_b[0] * field_b[0] + field_b[1] * field_b[1] + field_b[2] * field_b[2] + 1.0
    return (force_x * force_x + force_y * force_y + force_z * force_z) / strength + spread * spread


def stencil_kernel(
    place_ref, field_ref, y_low_ref, y_high_ref, z_low_ref, z_high_ref, corner_ref,
    grad_ref, loss_ref, wide, own, slopes,
):
    g, h = place_ref[0], place_ref[1]
    zero_rows = jnp.zeros((8, NX), F32)

    def kept(present, value):
        return jnp.where(present, value, jnp.zeros_like(value))

    for b in range(3):
        wide[b, 2:18, 8:24, :] = field_ref[b]
        wide[b, 0:2, 8:24, :] = kept(g > 0, y_low_ref[b])
        wide[b, 18:20, 8:24, :] = kept(g < GY - 1, y_high_ref[b])
        for plane in (0, 1, 18, 19):
            wide[b, plane, 0:8, :] = zero_rows
            wide[b, plane, 24:32, :] = zero_rows
        for y in range(LY):
            wide[b, y + 2, 0:8, :] = zero_rows
            wide[b, y + 2, 24:32, :] = zero_rows
            wide[b, y + 2, 6:8, :] = kept(h > 0, z_low_ref[b, 2 * y : 2 * y + 2, :])
            wide[b, y + 2, 24:26, :] = kept(h < GZ - 1, z_high_ref[b, 2 * y : 2 * y + 2, :])
        for index in range(4):
            y_side = g < GY - 1 if index // 2 else g > 0
            z_side = h < GZ - 1 if index % 2 else h > 0
            row = 24 if index % 2 else 7
            wide[b, 18 if index // 2 else 1, row : row + 1, :] = kept(
                jnp.logical_and(y_side, z_side), corner_ref[index, b : b + 1, :]
            )
    lane = lax.broadcasted_iota(jnp.int32, (32, NX), 1)
    row = lax.broadcasted_iota(jnp.int32, (32, NX), 0)
    z_cell = h * LZ + row - 8
    weight = jnp.where((z_cell >= 0) & (z_cell < NZ), 1.0 / CELLS, 0.0).astype(F32)
    inner = (row >= 8) & (row < 24)

    def x_diff(value):
        after = jnp.where(lane == NX - 1, 0.0, pltpu.roll(value, NX - 1, 1))
        before = jnp.where(lane == 0, 0.0, pltpu.roll(value, 1, 1))
        return (after - before) * 0.5

    def z_diff(value):
        return (pltpu.roll(value, 31, 0) - pltpu.roll(value, 1, 0)) * 0.5

    def one(plane, loss):
        cells = tuple(wide[b, plane] for b in range(3))
        slope_x = tuple(x_diff(value) for value in cells)
        slope_y = tuple((wide[b, plane + 1] - wide[b, plane - 1]) * 0.5 for b in range(3))
        slope_z = tuple(z_diff(value) for value in cells)
        terms, pullback = jax.vjp(cell_loss, cells, slope_x, slope_y, slope_z)
        y_cell = g * LY + plane - 2
        y_inside = jnp.logical_and(y_cell >= 0, y_cell < NY)
        grad_own, grad_x, grad_y, grad_z = pullback(jnp.where(y_inside, weight, 0.0))
        for b in range(3):
            own[b, plane - 1] = grad_own[b] - x_diff(grad_x[b]) - z_diff(grad_z[b])
            slopes[b, plane - 1] = grad_y[b]
        counted = jnp.logical_and(plane >= 2, plane < 18)
        return loss + jnp.where(jnp.logical_and(inner, counted), terms, 0.0)

    loss = lax.fori_loop(1, 19, one, jnp.zeros((32, NX), F32))
    total_loss = loss

    def finish(y, sums):
        result = []
        for b in range(3):
            grad = own[b, y + 1, 8:24, :] + (
                slopes[b, y, 8:24, :] - slopes[b, y + 2, 8:24, :]
            ) * 0.5
            grad_ref[b, y] = grad
            result.append(sums[b] + grad)
        return tuple(result)

    sums = lax.fori_loop(0, LY, finish, tuple(jnp.zeros((LZ, NX), F32) for _ in range(3)))
    loss_ref[...] = jnp.zeros_like(loss_ref)
    for index, value in enumerate((total_loss,) + sums):
        loss_ref[index : index + 1, :] = jnp.sum(value, axis=0, keepdims=True)


def stencil(place, field, *halos):
    vmem = pl.BlockSpec(memory_space=pltpu.VMEM)
    return pl.pallas_call(
        stencil_kernel,
        in_specs=[pl.BlockSpec(memory_space=pltpu.SMEM)] + [vmem] * 6,
        out_specs=[vmem] * 2,
        out_shape=[
            jax.ShapeDtypeStruct((3, LY, LZ, NX), F32),
            jax.ShapeDtypeStruct((8, NX), F32),
        ],
        scratch_shapes=[
            pltpu.VMEM((3, 20, 32, NX), F32),
            pltpu.VMEM((3, 18, 32, NX), F32),
            pltpu.VMEM((3, 18, 32, NX), F32),
        ],
        compiler_params=params(),
        name="stencil",
    )(place, field, *halos)


def on_device(field_in, spectral_weight, point_weight, point_bias, out_weight, out_bias):
    place = jnp.stack([lax.axis_index("gy"), lax.axis_index("gz")]).astype(jnp.int32)
    cells, rows, odd = x_transform(field_in)
    rows, odd = swap("gy", GY, 1, (FAR, NEAR), ("swap", rows), ("to0", odd))
    modes_in = to_kx(to_modes(2, SCALE, rows, odd).astype(BF16))

    mixed = jnp.einsum(
        "abkpi,abkio->abkpo", modes_in, spectral_weight, preferred_element_type=F32
    )
    real = mixed[..., 0, :C] - mixed[..., 1, C:]
    imag = mixed[..., 0, C:] + mixed[..., 1, :C]
    modes_out = jnp.stack([real, imag], axis=3)

    rows, odd = from_modes(4, from_kx(modes_out))
    rows, odd = swap("gy", GY, 6, (NEAR, FAR), ("swap", rows), ("from0", odd))

    hidden, slope, field_b, *edges = dense(
        rows, odd, cells, point_weight, point_bias, out_weight, out_bias
    )
    grad_b, loss_rows = stencil(place, field_b, *halo(10, field_b, *edges))
    rows, odd, small = grad_dense(hidden, slope, cells, grad_b, out_weight, loss_rows)
    small = small.reshape(GY, 8, 128)
    rows, odd, small = swap("gy", GY, 7, (FAR, NEAR), ("swap", rows), ("to0", odd), ("swap", small))
    dealt, small = to_modes(8, 1.0, rows, odd, small)
    small = small.reshape(128, 128)
    grad_modes = to_kx(dealt.astype(BF16))
    grad_spectral = weight_grad(modes_in, grad_modes).reshape(4, 2, M, C, 2 * C)
    scalars = jnp.sum(small[80:84], axis=1)
    return (
        scalars[0] / CELLS,
        grad_spectral,
        small[:C, :C],
        small[64, :C],
        small[72:75, :C].T,
        scalars[1:4],
    )


def solution(mesh):
    return jax.shard_map(
        on_device,
        mesh=mesh,
        in_specs=(P(None, "gy", "gz", None), P("gz", "gy", None, None, None), P(), P(), P(), P()),
        out_specs=(P(), P("gz", "gy", None, None, None), P(), P(), P(), P()),
        check_vma=False,
    )
```
